512 devices in a mesh: fib: 64 (over z, x, core), pln: 8 (over y).
Axes of the slice: x: 4, y: 8, z: 8, core: 2. Of those that a mesh axis runs over, the one named last changes fastest.
Arguments:
- nodal_values: float32 [8, 64, 288, 1000], P('pln', 'fib'), may hold values from -6 to 6
- interp_matrix: float32 [1000, 512], replicated, may hold values from -0.1875 to 0.1875
- count_table: int32 [8, 64, 3], P('pln'), may hold values from 1 to 96, as said below
- slot_order: int32 [8, 64, 192], P('pln', 'fib'), may hold values from 0 to 191, each once within a row
- start_basis: float32 [768, 128], replicated, may hold values from -6 to 6
Outputs:
- core_values: float32 [8, 64, 128, 128], P('pln', 'fib')
The draws below stay inside these ranges and needn't reach their ends.
Inputs may be any that keep to these rules, and one draw needn't show every extreme that they name: count_table[j, o, d] elements of owner o come from the source d places before it along fib, cyclically; for every owner the 3 entries sum to 192 and one equals 96. `slot_order`: each owner's row is a permutation.
All inputs are finite; a program needn't handle non-finite values.
Results may differ from the reference program's by a relative error of at most 0.0003.
Values sent between devices are 32-bit elements; how exact they have to be, the bound alone decides.
A program may use at most 64 MiB of HBM per device.

```python
import jax
import jax.numpy as jnp
from jax import lax

NX = 768
Q = 1000
TILE = 128
RANK = 128
WINDOW = 3
GRID_PTS = 512
OWNERS = 64
SLABS = 8
XB = 12
TT = 64
R_ELEM = 192
CAP = 96
E_SLOTS = 288


def draw_count_table(key, part):
    first_share = jax.random.randint(jax.random.fold_in(key, 11), (SLABS, OWNERS), 1, CAP)
    shares = jnp.stack([jnp.full((SLABS, OWNERS), CAP, jnp.int32), first_share, CAP - first_share], axis=-1)
    rotation = jax.random.randint(jax.random.fold_in(key, 12), (SLABS, OWNERS, 1), 0, WINDOW)
    ordering = (jnp.arange(WINDOW, dtype=jnp.int32)[None, None, :] + rotation) % WINDOW
    return jnp.take_along_axis(shares, ordering, axis=-1).astype(jnp.int32)


def shard_levels(own_key, dims, pieces, least, largest):
    gain = 1.0
    for axis_at, shards_of in pieces:
        heights = jax.random.uniform(jax.random.fold_in(jax.random.fold_in(own_key, 6), axis_at), (shards_of,), jnp.float32, least / len(pieces), largest / len(pieces))
        gain = gain * jnp.repeat(jnp.exp(heights), dims[axis_at] // shards_of).reshape((-1,) + (1,) * (len(dims) - 1 - axis_at))
    return gain


def noise(stream_key, extent, scale, reach, split=(), kind=jnp.bfloat16):
    gain = shard_levels(stream_key, extent, split, -0.22, 0.18) if split else 1.0
    drawn = jax.random.normal(stream_key, extent, jnp.float32) * scale * gain
    return jnp.minimum(jnp.maximum(drawn, -reach), reach).astype(kind)


def setup_inputs(seed: int = 0) -> dict:
    splits = jax.random.split(jax.random.key(seed), 6)
    nodal_values = noise(splits[0], (SLABS, OWNERS, E_SLOTS, Q), 1.0, 6.0, ((0, 8), (1, 64)), jnp.float32)
    interp_matrix = noise(splits[1], (Q, GRID_PTS), Q ** -0.5, 0.1875, (), jnp.float32)
    count_table = draw_count_table(jax.random.fold_in(splits[5], 71), 0)
    slot_order = jax.vmap(lambda own: jax.random.permutation(own, R_ELEM))(jax.random.split(splits[3], SLABS * OWNERS)).reshape((SLABS, OWNERS, R_ELEM)).astype(jnp.int32)
    start_basis = noise(splits[4], (NX, RANK), 1.0, 6.0, (), jnp.float32)
    return {"nodal_values": nodal_values, "interp_matrix": interp_matrix, "count_table": count_table, "slot_order": slot_order, "start_basis": start_basis}


def arrival_index(owner_table):
    sent_counts = jnp.stack([jnp.roll(owner_table[:, distance], -distance) for distance in range(WINDOW)], axis=1)
    starts = jnp.cumsum(sent_counts, axis=1) - sent_counts
    positions = jnp.arange(R_ELEM, dtype=jnp.int32)[None, :]
    owner_ids = jnp.arange(OWNERS, dtype=jnp.int32)[:, None]
    source_id = jnp.zeros((OWNERS, R_ELEM), jnp.int32)
    slot_id = jnp.zeros((OWNERS, R_ELEM), jnp.int32)
    offset = jnp.zeros((OWNERS, 1), jnp.int32)
    for distance in range(WINDOW - 1, -1, -1):
        taken_count = owner_table[:, distance:distance + 1].astype(jnp.int32)
        slot_begin = jnp.roll(starts[:, distance], distance)[:, None].astype(jnp.int32)
        inside = (positions >= offset) & (positions < offset + taken_count)
        source_id = jnp.where(inside, (owner_ids - distance) % OWNERS, source_id)
        slot_id = jnp.where(inside, slot_begin + positions - offset, slot_id)
        offset = offset + taken_count
    return (source_id.astype(jnp.int32), slot_id.astype(jnp.int32))

def reference(nodal_values, interp_matrix, count_table, slot_order, start_basis):
    full_precision = lax.Precision.HIGHEST

    def slab_field(operands):
        slab_nodes, owner_table, brick_order = operands
        source_id, slot_id = arrival_index(owner_table)
        gathered = slab_nodes[source_id, slot_id]
        grid_values = jnp.dot(gathered.reshape(-1, Q).astype(jnp.float32), interp_matrix.astype(jnp.float32), precision=full_precision, preferred_element_type=jnp.float32).reshape(OWNERS, R_ELEM, GRID_PTS)
        owner_ids = jnp.arange(OWNERS, dtype=jnp.int32)[:, None]
        brick_values = jnp.zeros_like(grid_values).at[owner_ids, brick_order].set(grid_values)
        fibre_field = brick_values.reshape(OWNERS, TT, XB, TILE).transpose(1, 0, 2, 3).reshape(TT, NX, TILE)
        gram_part = jnp.einsum('txf,tyf->xy', fibre_field, fibre_field, precision=full_precision)
        return (fibre_field, gram_part)
    fields, grams = lax.map(slab_field, (nodal_values, count_table, slot_order))
    gram_matrix = jnp.sum(grams, axis=0)
    image_matrix = jnp.dot(gram_matrix, start_basis, precision=full_precision)
    normal_matrix = jnp.dot(image_matrix.T, image_matrix, precision=full_precision)
    lower_factor = jnp.linalg.cholesky(normal_matrix)
    new_basis = jax.scipy.linalg.solve_triangular(lower_factor, image_matrix.T, lower=True).T
    core_values = jnp.einsum('xk,jtxf->jtkf', new_basis, fields, precision=full_precision)
    return core_values
```

```python
import functools

import jax
import jax.numpy as jnp
from jax import lax
from jax.experimental import pallas as pl
from jax.experimental.pallas import tpu as pltpu
from jax.sharding import PartitionSpec as P

NX = 768
RANK = 128
HIGHEST = lax.Precision.HIGHEST


def shifted(value, axis, by):
    peers = lax.axis_size(axis)
    return lax.ppermute(value, axis, [(i, (i + by) % peers) for i in range(peers)])


def eliminate_kernel(normal_ref, right_ref, out_ref):
    blocks = RANK // 8
    left = [normal_ref[8 * m:8 * m + 8, :] for m in range(blocks)]
    right = [right_ref[8 * m:8 * m + 8, :] for m in range(blocks)]
    rows = lax.broadcasted_iota(jnp.int32, (8, RANK), 0)
    for k in range(RANK):
        i, r = divmod(k, 8)
        row_left = left[i][r:r + 1, :]
        row_right = right[i][r:r + 1, :]
        pivot = row_left[:, k:k + 1]
        inverse = 1.0 / pivot
        scaled_left = row_left * inverse
        scaled_right = row_right * inverse
        out_ref[k:k + 1, :] = row_right * lax.rsqrt(pivot)
        for m in range(i, blocks):
            factor = jnp.broadcast_to(left[m][:, k:k + 1], (8, RANK))
            if m == i:
                factor = jnp.where(rows > r, factor, 0.0)
            left[m] = left[m] - factor * scaled_left
            right[m] = right[m] - factor * scaled_right


def eliminate(normal, right):
    return pl.pallas_call(
        eliminate_kernel,
        out_shape=jax.ShapeDtypeStruct((RANK, right.shape[1]), jnp.float32),
        in_specs=[pl.BlockSpec(memory_space=pltpu.VMEM)] * 2,
        out_specs=pl.BlockSpec(memory_space=pltpu.VMEM),
    )(normal, right)


def per_device(nodal_values, interp_matrix, count_table, slot_order, start_basis):
    node_rows = nodal_values[0, 0]
    owner_table = count_table[0]
    brick_order = slot_order[0, 0]
    owners = lax.axis_size("fib")
    own_index = lax.axis_index("fib")
    window = owner_table.shape[1]
    capacity = node_rows.shape[0] // window
    elements = brick_order.shape[0]
    block_width = NX // owners
    send_start = []
    running = jnp.int32(0)
    for distance in range(window):
        send_start.append(running)
        column = owner_table[:, distance]
        running = running + lax.dynamic_index_in_dim(
            column, (own_index + distance) % owners, 0, keepdims=False
        )
    own_counts = lax.dynamic_index_in_dim(owner_table, own_index, 0, keepdims=False)
    positions = jnp.arange(elements, dtype=jnp.int32)
    combined_index = jnp.zeros((elements,), jnp.int32)
    offset = jnp.int32(0)
    for distance in range(window - 1, -1, -1):
        taken_count = own_counts[distance]
        inside = (positions >= offset) & (positions < offset + taken_count)
        combined_index = jnp.where(inside, distance * capacity + positions - offset, combined_index)
        offset = offset + taken_count
    brick_source = jnp.zeros((elements,), jnp.int32).at[brick_order].set(combined_index)
    grid_rows = jnp.dot(
        node_rows, interp_matrix, precision=HIGHEST, preferred_element_type=jnp.float32
    )
    received = []
    for distance in range(window):
        send_piece = lax.dynamic_slice_in_dim(grid_rows, send_start[distance], capacity, 0)
        if distance > 0:
            send_piece = shifted(send_piece, "fib", distance)
        received.append(send_piece)
    brick_values = jnp.concatenate(received, axis=0)[brick_source]
    brick_grid = brick_values.reshape(owners, block_width, brick_values.shape[1] // 4)
    fibre_field = lax.all_to_all(brick_grid, "fib", split_axis=0, concat_axis=1, tiled=True)
    field = fibre_field[0]
    coefficients = jnp.einsum("xf,xk->fk", field, start_basis, precision=HIGHEST)
    image = lax.psum(jnp.dot(field, coefficients, precision=HIGHEST), ("fib", "pln"))
    normal = jnp.einsum("xk,xl->kl", image, image, precision=HIGHEST)
    right = jnp.einsum("xk,xf->kf", image, field, precision=HIGHEST)
    core_values = eliminate(normal, right)
    return core_values[None, None]


def solution(mesh):
    placed = (P("pln", "fib", None, None), P(), P("pln", None, None), P("pln", "fib", None), P())
    return jax.shard_map(
        per_device,
        mesh=mesh,
        in_specs=placed,
        out_specs=P("pln", "fib", None, None),
        check_vma=False,
    )
```

```python
import functools

import jax
import jax.numpy as jnp
from jax import lax
from jax.experimental import pallas as pl
from jax.experimental.pallas import tpu as pltpu
from jax.sharding import PartitionSpec as P

NX = 768
RANK = 128
HIGHEST = lax.Precision.HIGHEST


def shifted(value, axis, by):
    peers = lax.axis_size(axis)
    return lax.ppermute(value, axis, [(i, (i + by) % peers) for i in range(peers)])


def eliminate_kernel(normal_ref, right_ref, out_ref):
    blocks = RANK // 8
    left = [normal_ref[8 * m:8 * m + 8, :] for m in range(blocks)]
    right = [right_ref[8 * m:8 * m + 8, :] for m in range(blocks)]
    rows = lax.broadcasted_iota(jnp.int32, (8, RANK), 0)
    for k in range(RANK):
        i, r = divmod(k, 8)
        row_left = left[i][r:r + 1, :]
        row_right = right[i][r:r + 1, :]
        pivot = row_left[:, k:k + 1]
        inverse = 1.0 / pivot
        scaled_left = row_left * inverse
        scaled_right = row_right * inverse
        out_ref[k:k + 1, :] = row_right * lax.rsqrt(pivot)
        for m in range(i, blocks):
            factor = jnp.broadcast_to(left[m][:, k:k + 1], (8, RANK))
            if m == i:
                factor = jnp.where(rows > r, factor, 0.0)
            left[m] = left[m] - factor * scaled_left
            right[m] = right[m] - factor * scaled_right


def eliminate(normal, right):
    return pl.pallas_call(
        eliminate_kernel,
        out_shape=jax.ShapeDtypeStruct((RANK, right.shape[1]), jnp.float32),
        in_specs=[pl.BlockSpec(memory_space=pltpu.VMEM)] * 2,
        out_specs=pl.BlockSpec(memory_space=pltpu.VMEM),
    )(normal, right)


MESH_ID = pl.DeviceIdType.MESH
X_CHIPS = 4


class Place:
    def __init__(self, fib_size, pln_size):
        self.chips = fib_size // 2
        self.planes = pln_size
        self.fib = lax.axis_index("fib")
        self.pln = lax.axis_index("pln")
        self.core = lax.rem(self.fib, 2)
        self.chip = lax.div(self.fib, 2)
        self.z = lax.div(self.chip, X_CHIPS)
        self.x = lax.rem(self.chip, X_CHIPS)

    def other_core(self):
        return {"fib": self.chip * 2 + 1 - self.core, "pln": self.pln}

    def chip_at(self, step):
        z = lax.rem(self.z + lax.div(step, X_CHIPS), self.chips // X_CHIPS)
        x = lax.rem(self.x + lax.rem(step, X_CHIPS), X_CHIPS)
        return z * X_CHIPS + x

    def chip_before(self, step):
        depth = self.chips // X_CHIPS
        z = lax.rem(self.z + depth - lax.div(step, X_CHIPS), depth)
        x = lax.rem(self.x + X_CHIPS - lax.rem(step, X_CHIPS), X_CHIPS)
        return z * X_CHIPS + x

    def on_chip(self, chip):
        return {"fib": chip * 2 + self.core, "pln": self.pln}

    def in_plane(self, step):
        return {"fib": self.fib, "pln": lax.rem(self.pln + step, self.planes)}


def remote(src, dst, send_sem, recv_sem, device):
    return pltpu.make_async_remote_copy(
        src_ref=src, dst_ref=dst, send_sem=send_sem, recv_sem=recv_sem,
        device_id=device, device_id_type=MESH_ID,
    )


def loop(low, high, body):
    def step(i, carry):
        body(i)
        return carry
    lax.fori_loop(low, high, step, 0)


def reduce_kernel(fib_size, pln_size, field_ref, basis_ref, image_ref, part, other, half, chip_parts,
                  chunk_sum, plane_parts, chunk_done, core_sems, chip_send, chip_recv, plane_send,
                  plane_recv, gather_send, gather_recv, relay_send, relay_recv):
    at = Place(fib_size, pln_size)
    chips, planes = at.chips, at.planes
    size = NX // 4 // 2 // chips
    split = size * chips
    barrier = pltpu.get_barrier_semaphore()

    def greet(device):
        pl.semaphore_signal(barrier, inc=1, device_id=device, device_id_type=MESH_ID)

    greet(at.other_core())
    loop(1, chips, lambda i: greet(at.on_chip(at.chip_at(i))))
    loop(1, planes, lambda i: greet(at.in_plane(i)))

    field = field_ref[...]
    coefficients = lax.dot_general(
        field, basis_ref[...], (((0,), (0,)), ((), ())), precision=HIGHEST,
        preferred_element_type=jnp.float32)
    product = jnp.dot(field, coefficients, precision=HIGHEST, preferred_element_type=jnp.float32)
    part[...] = product.reshape(NX // 4, 4, RANK)

    pl.semaphore_wait(barrier, chips + planes - 1)

    swap = remote(part.at[pl.ds((1 - at.core) * split, split)], other, core_sems.at[0], core_sems.at[1],
                  at.other_core())
    swap.start()
    swap.wait()
    half[...] = part[pl.ds(at.core * split, split)] + other[...]

    def send_chunk(i):
        chip = at.chip_at(i)
        remote(half.at[pl.ds(chip * size, size)], chip_parts.at[i], chip_send.at[i], chip_recv.at[i],
               at.on_chip(chip)).start()

    def chunk_copy(i):
        return remote(half.at[pl.ds(0, size)], chip_parts.at[i], chip_send.at[i], chip_recv.at[i],
                      at.on_chip(at.chip_at(i)))

    loop(1, chips, send_chunk)
    chunk_sum[...] = half[pl.ds(at.chip * size, size)]

    def add_chunk(i):
        chunk_copy(i).wait_recv()
        chunk_sum[...] += chip_parts[i]

    loop(1, chips, add_chunk)

    def plane_copy(i):
        return remote(chunk_sum, plane_parts.at[i], plane_send.at[i], plane_recv.at[i], at.in_plane(i))

    loop(1, planes, lambda i: plane_copy(i).start())
    chunk_done[...] = chunk_sum[...]

    def add_plane(i):
        plane_copy(i).wait_recv()
        chunk_done[...] += plane_parts[i]

    loop(1, planes, add_plane)

    def place_of(chip):
        return pl.ds(at.core * split + chip * size, size)

    def gather_copy(i):
        return remote(chunk_done, image_ref.at[place_of(at.chip)], gather_send.at[i], gather_recv.at[i],
                      at.on_chip(at.chip_at(i)))

    def relay_copy(i, source):
        return remote(source, image_ref.at[place_of(at.chip_before(i))], relay_send.at[i], relay_recv.at[i],
                      at.other_core())

    loop(1, chips, lambda i: gather_copy(i).start())
    relay_copy(0, chunk_done).start()
    image_ref[place_of(at.chip)] = chunk_done[...]

    def pass_on(i):
        gather_copy(i).wait_recv()
        relay_copy(i, image_ref.at[place_of(at.chip_before(i))]).start()

    loop(1, chips, pass_on)
    loop(0, chips, lambda i: relay_copy(i, chunk_done).wait())
    loop(1, chips, lambda i: chunk_copy(i).wait_send())
    loop(1, planes, lambda i: plane_copy(i).wait_send())
    loop(1, chips, lambda i: gather_copy(i).wait_send())


def summed_image(field, basis, fib_size, pln_size):
    chips = fib_size // 2
    size = NX // 4 // 2 // chips
    vmem = lambda *shape: pltpu.VMEM(shape, jnp.float32)
    dma = lambda n: pltpu.SemaphoreType.DMA((n,))
    image = pl.pallas_call(
        functools.partial(reduce_kernel, fib_size, pln_size),
        out_shape=jax.ShapeDtypeStruct((NX // 4, 4, RANK), jnp.float32),
        in_specs=[pl.BlockSpec(memory_space=pltpu.VMEM)] * 2,
        out_specs=pl.BlockSpec(memory_space=pltpu.VMEM),
        scratch_shapes=[
            vmem(NX // 4, 4, RANK), vmem(size * chips, 4, RANK), vmem(size * chips, 4, RANK),
            vmem(chips, size, 4, RANK), vmem(size, 4, RANK), vmem(pln_size, size, 4, RANK),
            vmem(size, 4, RANK),
            dma(2), dma(chips), dma(chips), dma(pln_size), dma(pln_size), dma(chips), dma(chips),
            dma(chips), dma(chips),
        ],
        compiler_params=pltpu.CompilerParams(collective_id=0, has_side_effects=True),
    )(field, basis)
    return image.reshape(NX, RANK)


def per_device(nodal_values, interp_matrix, count_table, slot_order, start_basis):
    node_rows = nodal_values[0, 0]
    owner_table = count_table[0]
    brick_order = slot_order[0, 0]
    owners = lax.axis_size("fib")
    own_index = lax.axis_index("fib")
    window = owner_table.shape[1]
    capacity = node_rows.shape[0] // window
    elements = brick_order.shape[0]
    block_width = NX // owners
    send_start = []
    running = jnp.int32(0)
    for distance in range(window):
        send_start.append(running)
        column = owner_table[:, distance]
        running = running + lax.dynamic_index_in_dim(
            column, (own_index + distance) % owners, 0, keepdims=False
        )
    own_counts = lax.dynamic_index_in_dim(owner_table, own_index, 0, keepdims=False)
    positions = jnp.arange(elements, dtype=jnp.int32)
    combined_index = jnp.zeros((elements,), jnp.int32)
    offset = jnp.int32(0)
    for distance in range(window - 1, -1, -1):
        taken_count = own_counts[distance]
        inside = (positions >= offset) & (positions < offset + taken_count)
        combined_index = jnp.where(inside, distance * capacity + positions - offset, combined_index)
        offset = offset + taken_count
    brick_source = jnp.zeros((elements,), jnp.int32).at[brick_order].set(combined_index)
    grid_rows = jnp.dot(
        node_rows, interp_matrix, precision=HIGHEST, preferred_element_type=jnp.float32
    )
    received = []
    for distance in range(window):
        send_piece = lax.dynamic_slice_in_dim(grid_rows, send_start[distance], capacity, 0)
        if distance > 0:
            send_piece = shifted(send_piece, "fib", distance)
        received.append(send_piece)
    brick_values = jnp.concatenate(received, axis=0)[brick_source]
    brick_grid = brick_values.reshape(owners, block_width, brick_values.shape[1] // 4)
    fibre_field = lax.all_to_all(brick_grid, "fib", split_axis=0, concat_axis=1, tiled=True)
    field = fibre_field[0]
    image = summed_image(field, start_basis, owners, lax.axis_size("pln"))
    normal = jnp.einsum("xk,xl->kl", image, image, precision=HIGHEST)
    right = jnp.einsum("xk,xf->kf", image, field, precision=HIGHEST)
    core_values = eliminate(normal, right)
    return core_values[None, None]


def solution(mesh):
    placed = (P("pln", "fib", None, None), P(), P("pln", None, None), P("pln", "fib", None), P())
    return jax.shard_map(
        per_device,
        mesh=mesh,
        in_specs=placed,
        out_specs=P("pln", "fib", None, None),
        check_vma=False,
    )
```

```python
import functools

import jax
import jax.numpy as jnp
from jax import lax
from jax.experimental import pallas as pl
from jax.experimental.pallas import tpu as pltpu
from jax.sharding import PartitionSpec as P

NX = 768
RANK = 128
HIGHEST = lax.Precision.HIGHEST


WINDOW = 3
CAP = 96
R_ELEM = 192
PIECES = NX // 4


def eliminate_kernel(image_ref, field_ref, out_ref):
    blocks = RANK // 8
    image = image_ref[...]

    def against_image(other):
        return lax.dot_general(image, other, (((0,), (0,)), ((), ())), precision=HIGHEST,
                               preferred_element_type=jnp.float32)

    normal = against_image(image)
    product = against_image(field_ref[...])
    left = [normal[8 * m:8 * m + 8, :] for m in range(blocks)]
    right = [product[8 * m:8 * m + 8, :] for m in range(blocks)]
    rows = lax.broadcasted_iota(jnp.int32, (8, RANK), 0)
    for k in range(RANK):
        i, r = divmod(k, 8)
        row_left = left[i][r:r + 1, :]
        row_right = right[i][r:r + 1, :]
        pivot = row_left[:, k:k + 1]
        inverse = 1.0 / pivot
        scaled_left = row_left * inverse
        scaled_right = row_right * inverse
        out_ref[k:k + 1, :] = row_right * lax.rsqrt(pivot)
        for m in range(i, blocks):
            factor = jnp.broadcast_to(left[m][:, k:k + 1], (8, RANK))
            if m == i:
                factor = jnp.where(rows > r, factor, 0.0)
            left[m] = left[m] - factor * scaled_left
            right[m] = right[m] - factor * scaled_right


def eliminate(image, field):
    return pl.pallas_call(
        eliminate_kernel,
        out_shape=jax.ShapeDtypeStruct((RANK, field.shape[1]), jnp.float32),
        in_specs=[pl.BlockSpec(memory_space=pltpu.VMEM)] * 2,
        out_specs=pl.BlockSpec(memory_space=pltpu.VMEM),
    )(image, field)


MESH_ID = pl.DeviceIdType.MESH
X_CHIPS = 4


class Place:
    def __init__(self, fib_size, pln_size):
        self.chips = fib_size // 2
        self.planes = pln_size
        self.fib = lax.axis_index("fib")
        self.pln = lax.axis_index("pln")
        self.core = lax.rem(self.fib, 2)
        self.chip = lax.div(self.fib, 2)
        self.z = lax.div(self.chip, X_CHIPS)
        self.x = lax.rem(self.chip, X_CHIPS)

    def other_core(self):
        return {"fib": self.chip * 2 + 1 - self.core, "pln": self.pln}

    def chip_at(self, step):
        z = lax.rem(self.z + lax.div(step, X_CHIPS), self.chips // X_CHIPS)
        x = lax.rem(self.x + lax.rem(step, X_CHIPS), X_CHIPS)
        return z * X_CHIPS + x

    def chip_before(self, step):
        depth = self.chips // X_CHIPS
        z = lax.rem(self.z + depth - lax.div(step, X_CHIPS), depth)
        x = lax.rem(self.x + X_CHIPS - lax.rem(step, X_CHIPS), X_CHIPS)
        return z * X_CHIPS + x

    def along(self, step):
        core = lax.rem(self.core + lax.rem(step, 2), 2)
        return self.chip_at(lax.div(step, 2)) * 2 + core

    def after(self, distance):
        return lax.rem(self.fib + distance, 2 * self.chips)

    def in_fib(self, fib):
        return {"fib": fib, "pln": self.pln}

    def on_chip(self, chip):
        return {"fib": chip * 2 + self.core, "pln": self.pln}

    def in_plane(self, step):
        return {"fib": self.fib, "pln": lax.rem(self.pln + step, self.planes)}


def remote(src, dst, send_sem, recv_sem, device):
    return pltpu.make_async_remote_copy(
        src_ref=src, dst_ref=dst, send_sem=send_sem, recv_sem=recv_sem,
        device_id=device, device_id_type=MESH_ID,
    )


def loop(low, high, body):
    def step(i, carry):
        body(i)
        return carry
    lax.fori_loop(low, high, step, 0)


def pair(value):
    high = value.astype(jnp.bfloat16)
    return high, (value - high.astype(jnp.float32)).astype(jnp.bfloat16)


def mult(left, right):
    return jnp.dot(left, right, preferred_element_type=jnp.float32)


def step_kernel(fib_size, pln_size, nodes_ref, interp_ref, table_ref, order_ref, basis_ref, field_ref, image_ref,
                outgoing, incoming, brick, part, other, half, chip_parts, chunk_sum, plane_parts, chunk_done,
                shift_send, shift_recv, tile_send, tile_recv, core_sems, chip_send, chip_recv, plane_send,
                plane_recv, gather_send, gather_recv, relay_send, relay_recv):
    at = Place(fib_size, pln_size)
    chips, planes = at.chips, at.planes
    size = PIECES // 2 // chips
    split = size * chips
    run = PIECES // fib_size
    barrier = pltpu.get_barrier_semaphore()

    def greet(device):
        pl.semaphore_signal(barrier, inc=1, device_id=device, device_id_type=MESH_ID)

    loop(1, fib_size, lambda i: greet(at.in_fib(at.along(i))))
    loop(1, planes, lambda i: greet(at.in_plane(i)))

    starts = [0]
    for distance in range(WINDOW - 1):
        starts.append(starts[-1] + table_ref[at.after(distance), distance])
    interp_high, interp_low = pair(interp_ref[...])
    nodes_high, nodes_low = pair(nodes_ref[...])
    slots = (lax.broadcasted_iota(jnp.int32, (CAP, WINDOW * CAP), 1)
             - lax.broadcasted_iota(jnp.int32, (CAP, WINDOW * CAP), 0))

    def shift_copy(distance):
        return remote(outgoing.at[distance - 1], incoming.at[distance], shift_send.at[distance - 1],
                      shift_recv.at[distance - 1], at.in_fib(at.after(distance)))

    for distance in range(WINDOW - 1, -1, -1):
        if distance == 0:
            high, low = nodes_high[:CAP], nodes_low[:CAP]
        else:
            window = jnp.where(slots == starts[distance], 1.0, 0.0).astype(jnp.bfloat16)
            high = mult(window, nodes_high).astype(jnp.bfloat16)
            low = mult(window, nodes_low).astype(jnp.bfloat16)
        values = mult(high, interp_high) + (mult(high, interp_low) + mult(low, interp_high))
        if distance == 0:
            incoming[0] = values
        else:
            outgoing[distance - 1] = values
            if distance == WINDOW - 1:
                pl.semaphore_wait(barrier, fib_size + planes - 2)
            shift_copy(distance).start()

    taken_near = table_ref[at.fib, 1]
    taken_far = table_ref[at.fib, 2]
    ranks = lax.broadcasted_iota(jnp.int32, (1, R_ELEM), 1)
    source = jnp.where(ranks < taken_far, 2 * CAP + ranks,
                       jnp.where(ranks < taken_far + taken_near, CAP + ranks - taken_far,
                                 ranks - taken_far - taken_near))
    places = lax.broadcasted_iota(jnp.int32, (R_ELEM, R_ELEM), 0)
    chosen = jnp.where(order_ref[...] == places, source.astype(jnp.float32), 0.0)
    chosen = jnp.sum(chosen, axis=1, keepdims=True).astype(jnp.int32)
    select = lax.broadcasted_iota(jnp.int32, (R_ELEM, WINDOW * CAP), 1) == chosen
    select = jnp.where(select, 1.0, 0.0).astype(jnp.bfloat16)
    for distance in range(1, WINDOW):
        shift_copy(distance).wait_recv()
    rows = incoming[...].reshape(WINDOW * CAP, 4 * RANK)
    high, low = pair(rows)
    rest = (rows - high.astype(jnp.float32)) - low.astype(jnp.float32)
    values = mult(select, high) + (mult(select, low) + mult(select, rest.astype(jnp.bfloat16)))
    for l in range(4):
        brick[:, l, :] = values[:, l * RANK:(l + 1) * RANK]

    def own_pieces(fib):
        return pl.ds(fib * run, run)

    def tile_copy(i):
        peer = at.along(i)
        return remote(brick.at[own_pieces(peer)], field_ref.at[own_pieces(at.fib)], tile_send.at[i],
                      tile_recv.at[i], at.in_fib(peer))

    loop(1, fib_size, lambda i: tile_copy(i).start())
    field_ref[own_pieces(at.fib)] = brick[own_pieces(at.fib)]
    loop(1, fib_size, lambda i: tile_copy(i).wait_recv())

    field = field_ref[...].reshape(NX, RANK)
    coefficients = lax.dot_general(
        field, basis_ref[...], (((0,), (0,)), ((), ())), precision=HIGHEST,
        preferred_element_type=jnp.float32)
    product = jnp.dot(field, coefficients, precision=HIGHEST, preferred_element_type=jnp.float32)
    part[...] = product.reshape(PIECES, 4, RANK)

    swap = remote(part.at[pl.ds((1 - at.core) * split, split)], other, core_sems.at[0], core_sems.at[1],
                  at.other_core())
    swap.start()
    swap.wait()
    half[...] = part[pl.ds(at.core * split, split)] + other[...]

    def send_chunk(i):
        chip = at.chip_at(i)
        remote(half.at[pl.ds(chip * size, size)], chip_parts.at[i], chip_send.at[i], chip_recv.at[i],
               at.on_chip(chip)).start()

    def chunk_copy(i):
        return remote(half.at[pl.ds(0, size)], chip_parts.at[i], chip_send.at[i], chip_recv.at[i],
                      at.on_chip(at.chip_at(i)))

    loop(1, chips, send_chunk)
    chunk_sum[...] = half[pl.ds(at.chip * size, size)]

    def add_chunk(i):
        chunk_copy(i).wait_recv()
        chunk_sum[...] += chip_parts[i]

    loop(1, chips, add_chunk)

    def plane_copy(i):
        return remote(chunk_sum, plane_parts.at[i], plane_send.at[i], plane_recv.at[i], at.in_plane(i))

    loop(1, planes, lambda i: plane_copy(i).start())
    chunk_done[...] = chunk_sum[...]

    def add_plane(i):
        plane_copy(i).wait_recv()
        chunk_done[...] += plane_parts[i]

    loop(1, planes, add_plane)

    def place_of(chip):
        return pl.ds(at.core * split + chip * size, size)

    def gather_copy(i):
        return remote(chunk_done, image_ref.at[place_of(at.chip)], gather_send.at[i], gather_recv.at[i],
                      at.on_chip(at.chip_at(i)))

    def relay_copy(i, source):
        return remote(source, image_ref.at[place_of(at.chip_before(i))], relay_send.at[i], relay_recv.at[i],
                      at.other_core())

    loop(1, chips, lambda i: gather_copy(i).start())
    relay_copy(0, chunk_done).start()
    image_ref[place_of(at.chip)] = chunk_done[...]

    def pass_on(i):
        gather_copy(i).wait_recv()
        relay_copy(i, image_ref.at[place_of(at.chip_before(i))]).start()

    loop(1, chips, pass_on)
    loop(0, chips, lambda i: relay_copy(i, chunk_done).wait())
    loop(1, chips, lambda i: chunk_copy(i).wait_send())
    loop(1, planes, lambda i: plane_copy(i).wait_send())
    loop(1, chips, lambda i: gather_copy(i).wait_send())
    loop(1, fib_size, lambda i: tile_copy(i).wait_send())
    for distance in range(1, WINDOW):
        shift_copy(distance).wait_send()


def field_and_image(nodes, interp, table, order, basis, fib_size, pln_size):
    chips = fib_size // 2
    size = PIECES // 2 // chips
    vmem = lambda *shape: pltpu.VMEM(shape, jnp.float32)
    dma = lambda n: pltpu.SemaphoreType.DMA((n,))
    whole = pl.BlockSpec(memory_space=pltpu.VMEM)
    pieces = jax.ShapeDtypeStruct((PIECES, 4, RANK), jnp.float32)
    field, image = pl.pallas_call(
        functools.partial(step_kernel, fib_size, pln_size),
        out_shape=(pieces, pieces),
        in_specs=[whole, whole, pl.BlockSpec(memory_space=pltpu.SMEM), whole, whole],
        out_specs=(whole, whole),
        scratch_shapes=[
            vmem(WINDOW - 1, CAP, 4 * RANK), vmem(WINDOW, CAP, 4 * RANK), vmem(PIECES, 4, RANK),
            vmem(PIECES, 4, RANK), vmem(size * chips, 4, RANK), vmem(size * chips, 4, RANK),
            vmem(chips, size, 4, RANK), vmem(size, 4, RANK), vmem(pln_size, size, 4, RANK),
            vmem(size, 4, RANK),
            dma(WINDOW - 1), dma(WINDOW - 1), dma(fib_size), dma(fib_size),
            dma(2), dma(chips), dma(chips), dma(pln_size), dma(pln_size), dma(chips), dma(chips),
            dma(chips), dma(chips),
        ],
        compiler_params=pltpu.CompilerParams(collective_id=0, has_side_effects=True),
    )(nodes, interp, table, order, basis)
    return field.reshape(NX, RANK), image.reshape(NX, RANK)


def per_device(nodal_values, interp_matrix, count_table, slot_order, start_basis):
    field, image = field_and_image(
        nodal_values[0, 0], interp_matrix, count_table[0], slot_order[0], start_basis,
        lax.axis_size("fib"), lax.axis_size("pln"))
    return eliminate(image, field)[None, None]


def solution(mesh):
    placed = (P("pln", "fib", None, None), P(), P("pln", None, None), P("pln", "fib", None), P())
    return jax.shard_map(
        per_device,
        mesh=mesh,
        in_specs=placed,
        out_specs=P("pln", "fib", None, None),
        check_vma=False,
    )
```

```python
import functools

import jax
import jax.numpy as jnp
from jax import lax
from jax.experimental import pallas as pl
from jax.experimental.pallas import tpu as pltpu
from jax.sharding import PartitionSpec as P

NX = 768
RANK = 128
WINDOW = 3
CAP = 96
R_ELEM = 192
PIECES = NX // 4
X_CHIPS = 4
CUTS = 4
PIVOTS = 4
HIGHEST = lax.Precision.HIGHEST
MESH_ID = pl.DeviceIdType.MESH


def eliminate_kernel(system_ref, out_ref):
    blocks = RANK // 8
    left = [system_ref[8 * m:8 * m + 8, :RANK] for m in range(blocks)]
    right = [system_ref[8 * m:8 * m + 8, RANK:] for m in range(blocks)]
    rows = lax.broadcasted_iota(jnp.int32, (8, RANK), 0)

    def spread(row):
        return jnp.broadcast_to(row, (8, RANK))

    for k in range(0, RANK, PIVOTS):
        i, r = divmod(k, 8)
        row_left = [spread(left[i][r + a:r + a + 1, :]) for a in range(PIVOTS)]
        row_right = [spread(right[i][r + a:r + a + 1, :]) for a in range(PIVOTS)]
        corner = [[spread(row_left[a][:, k + b:k + b + 1]) if b >= a else None for b in range(PIVOTS)]
                  for a in range(PIVOTS)]
        ratio = [[None] * PIVOTS for _ in range(PIVOTS)]
        inverse = []
        for a in range(PIVOTS):
            inverse.append(1.0 / corner[a][a])
            for b in range(a + 1, PIVOTS):
                ratio[a][b] = corner[a][b] * inverse[a]
                for c in range(b, PIVOTS):
                    corner[b][c] = corner[b][c] - ratio[a][b] * corner[a][c]
                row_left[b] = row_left[b] - ratio[a][b] * row_left[a]
                row_right[b] = row_right[b] - ratio[a][b] * row_right[a]
        for a in range(PIVOTS):
            out_ref[k + a:k + a + 1, :] = (row_right[a] * lax.rsqrt(corner[a][a]))[:1]
        scaled_left = [row_left[a] * inverse[a] for a in range(PIVOTS)]
        scaled_right = [row_right[a] * inverse[a] for a in range(PIVOTS)]
        for m in range(i if r + PIVOTS < 8 else i + 1, blocks):
            factor = []
            for a in range(PIVOTS):
                column = spread(left[m][:, k + a:k + a + 1])
                if m == i:
                    column = jnp.where(rows >= r + PIVOTS, column, 0.0)
                for b in range(a):
                    column = column - ratio[b][a] * factor[b]
                factor.append(column)
            for a in range(PIVOTS):
                left[m] = left[m] - factor[a] * scaled_left[a]
                right[m] = right[m] - factor[a] * scaled_right[a]


def eliminate(system):
    return pl.pallas_call(
        eliminate_kernel,
        out_shape=jax.ShapeDtypeStruct((RANK, system.shape[1] - RANK), jnp.float32),
        in_specs=[pl.BlockSpec(memory_space=pltpu.VMEM)],
        out_specs=pl.BlockSpec(memory_space=pltpu.VMEM),
    )(system)


def remote(src, dst, send_sem, recv_sem, device):
    return pltpu.make_async_remote_copy(
        src_ref=src, dst_ref=dst, send_sem=send_sem, recv_sem=recv_sem,
        device_id=device, device_id_type=MESH_ID,
    )


def loop(low, high, body):
    def step(i, carry):
        body(i)
        return carry
    lax.fori_loop(low, high, step, 0)


class Place:
    def __init__(self, fib_size, pln_size):
        self.fib_size = fib_size
        self.chips = fib_size // 2
        self.depth = self.chips // X_CHIPS
        self.planes = pln_size
        self.fib = lax.axis_index("fib")
        self.pln = lax.axis_index("pln")
        self.core = lax.rem(self.fib, 2)
        self.chip = lax.div(self.fib, 2)
        self.z = lax.div(self.chip, X_CHIPS)
        self.x = lax.rem(self.chip, X_CHIPS)
        self.x_after = [lax.rem(self.x + step, X_CHIPS) for step in range(X_CHIPS)]
        self.x_before = [lax.rem(self.x + X_CHIPS - step, X_CHIPS) for step in range(X_CHIPS)]

    def at_fib(self, fib):
        return {"fib": fib, "pln": self.pln}

    def on_chip(self, chip):
        return self.at_fib(chip * 2 + self.core)

    def other_core(self):
        return self.at_fib(self.chip * 2 + 1 - self.core)

    def after(self, distance):
        return lax.rem(self.fib + distance, self.fib_size)

    def in_plane(self, step):
        return {"fib": self.fib, "pln": lax.rem(self.pln + step, self.planes)}

    def over_depth(self, row, far_first):
        if far_first:
            skip = (self.depth // 2 - 2) % (self.depth - 1)
            loop(0, self.depth - 1, lambda n: row(lax.rem(n + skip, self.depth - 1) + 1, True))
            row(0, False)
        else:
            row(0, False)
            loop(1, self.depth, lambda n: row(n, True))

    def each_chip(self, body, far_first=False):
        def row(z_step, with_own):
            ahead = lax.rem(self.z + z_step, self.depth) * X_CHIPS
            behind = lax.rem(self.z + self.depth - z_step, self.depth) * X_CHIPS
            for x_step in range(0 if with_own else 1, X_CHIPS):
                body(z_step * X_CHIPS + x_step, ahead + self.x_after[x_step], behind + self.x_before[x_step])
        self.over_depth(row, far_first)

    def each_device(self, body, far_first=False):
        def row(z_step, with_own):
            ahead = lax.rem(self.z + z_step, self.depth) * X_CHIPS
            for x_step in range(X_CHIPS):
                for turn in range(2):
                    if with_own or x_step or turn:
                        core = self.core if turn == 0 else 1 - self.core
                        body((z_step * X_CHIPS + x_step) * 2 + turn, (ahead + self.x_after[x_step]) * 2 + core)
        self.over_depth(row, far_first)


def pair(value):
    high = value.astype(jnp.bfloat16)
    return high, (value - high.astype(jnp.float32)).astype(jnp.bfloat16)


def mult(left, right):
    return jnp.dot(left, right, preferred_element_type=jnp.float32)


def gram(left, right):
    return lax.dot_general(left, right, (((0,), (0,)), ((), ())), precision=HIGHEST,
                           preferred_element_type=jnp.float32)


def step_kernel(fib_size, pln_size, nodes_hbm, interp_hbm, table_ref, order_ref, basis_hbm, system_ref,
                nodes_ref, interp_ref, basis_ref, outgoing, incoming, brick, field_ref, image_ref, part, other,
                half, chip_parts, chunk_sum, plane_parts, chunk_done, load_sems, shift_send, shift_recv,
                tile_send, tile_recv, core_sems, chip_send, chip_recv, plane_send, plane_recv, gather_send,
                gather_recv, relay_send, relay_recv):
    at = Place(fib_size, pln_size)
    chips, planes = at.chips, at.planes
    size = PIECES // 2 // chips
    split = size * chips
    run = PIECES // fib_size
    barrier = pltpu.get_barrier_semaphore()
    loads = [pltpu.make_async_copy(nodes_hbm, nodes_ref, load_sems.at[0]),
             pltpu.make_async_copy(interp_hbm, interp_ref, load_sems.at[1]),
             pltpu.make_async_copy(basis_hbm, basis_ref, load_sems.at[2])]
    for load in loads:
        load.start()

    def greet(device):
        pl.semaphore_signal(barrier, inc=1, device_id=device, device_id_type=MESH_ID)

    at.each_device(lambda i, fib: greet(at.at_fib(fib)), far_first=True)
    loop(1, planes, lambda i: greet(at.in_plane(i)))

    starts = [0]
    for distance in range(WINDOW - 1):
        starts.append(starts[-1] + table_ref[distance, 0, at.after(distance)])
    slots = (lax.broadcasted_iota(jnp.int32, (CAP, WINDOW * CAP), 1)
             - lax.broadcasted_iota(jnp.int32, (CAP, WINDOW * CAP), 0))
    for load in loads:
        load.wait()
    interp_high, interp_low = pair(interp_ref[...])
    nodes_high, nodes_low = pair(nodes_ref[...])

    def shift_copies(distance):
        rows = CAP // CUTS
        return [remote(outgoing.at[distance - 1, pl.ds(cut * rows, rows)],
                       incoming.at[distance, pl.ds(cut * rows, rows)],
                       shift_send.at[distance - 1, cut], shift_recv.at[distance - 1, cut],
                       at.at_fib(at.after(distance))) for cut in range(CUTS)]

    for distance in range(WINDOW - 1, -1, -1):
        if distance == 0:
            high, low = nodes_high[:CAP], nodes_low[:CAP]
        else:
            window = jnp.where(slots == starts[distance], 1.0, 0.0).astype(jnp.bfloat16)
            high = mult(window, nodes_high).astype(jnp.bfloat16)
            low = mult(window, nodes_low).astype(jnp.bfloat16)
        values = mult(high, interp_high) + (mult(high, interp_low) + mult(low, interp_high))
        if distance == 0:
            incoming[0] = values
        else:
            outgoing[distance - 1] = values
            if distance == WINDOW - 1:
                pl.semaphore_wait(barrier, fib_size + planes - 2)
            for copy in shift_copies(distance):
                copy.start()

    taken_near = table_ref[1, 0, at.fib]
    taken_far = table_ref[2, 0, at.fib]
    ranks = lax.broadcasted_iota(jnp.int32, (1, R_ELEM), 1)
    source = jnp.where(ranks < taken_far, 2 * CAP + ranks,
                       jnp.where(ranks < taken_far + taken_near, CAP + ranks - taken_far,
                                 ranks - taken_far - taken_near))
    places = lax.broadcasted_iota(jnp.int32, (R_ELEM, R_ELEM), 0)
    chosen = jnp.where(order_ref[...] == places, source.astype(jnp.float32), 0.0)
    chosen = jnp.sum(chosen, axis=1, keepdims=True).astype(jnp.int32)
    select = lax.broadcasted_iota(jnp.int32, (R_ELEM, WINDOW * CAP), 1) == chosen
    select = jnp.where(select, 1.0, 0.0).astype(jnp.bfloat16)
    for distance in range(WINDOW - 1, 0, -1):
        for copy in shift_copies(distance):
            copy.wait_recv()
    rows = incoming[...].reshape(WINDOW * CAP, 4 * RANK)
    high, low = pair(rows)
    rest = (rows - high.astype(jnp.float32)) - low.astype(jnp.float32)
    values = mult(select, high) + (mult(select, low) + mult(select, rest.astype(jnp.bfloat16)))
    for l in range(4):
        brick[:, l, :] = values[:, l * RANK:(l + 1) * RANK]

    def own_pieces(fib):
        return pl.ds(fib * run, run)

    def tile_copy(i, peer):
        return remote(brick.at[own_pieces(peer)], field_ref.at[own_pieces(at.fib)], tile_send.at[i],
                      tile_recv.at[i], at.at_fib(peer))

    at.each_device(lambda i, peer: tile_copy(i, peer).start(), far_first=True)
    field_ref[own_pieces(at.fib)] = brick[own_pieces(at.fib)]
    loop(1, fib_size, lambda i: tile_copy(i, at.fib).wait_recv())

    field = field_ref[...].reshape(NX, RANK)
    product = jnp.dot(field, gram(field, basis_ref[...]), precision=HIGHEST,
                      preferred_element_type=jnp.float32)
    part[...] = product.reshape(PIECES, 4, RANK)

    swap = remote(part.at[pl.ds((1 - at.core) * split, split)], other, core_sems.at[0], core_sems.at[1],
                  at.other_core())
    swap.start()
    swap.wait()
    half[...] = part[pl.ds(at.core * split, split)] + other[...]

    def chunk_copy(i, chip):
        return remote(half.at[pl.ds(chip * size, size)], chip_parts.at[i], chip_send.at[i], chip_recv.at[i],
                      at.on_chip(chip))

    at.each_chip(lambda i, chip, back: chunk_copy(i, chip).start(), far_first=True)
    chunk_sum[...] = half[pl.ds(at.chip * size, size)]

    def add_chunk(i):
        chunk_copy(i, at.chip).wait_recv()
        chunk_sum[...] += chip_parts[i]

    loop(1, chips, add_chunk)

    def plane_copy(i):
        return remote(chunk_sum, plane_parts.at[i], plane_send.at[i], plane_recv.at[i], at.in_plane(i))

    loop(1, planes, lambda i: plane_copy(i).start())
    chunk_done[...] = chunk_sum[...]

    def add_plane(i):
        plane_copy(i).wait_recv()
        chunk_done[...] += plane_parts[i]

    loop(1, planes, add_plane)

    def place_of(chip):
        return pl.ds(at.core * split + chip * size, size)

    def gather_copy(i, chip):
        return remote(chunk_done, image_ref.at[place_of(at.chip)], gather_send.at[i], gather_recv.at[i],
                      at.on_chip(chip))

    def relay_copy(i, source, chip):
        return remote(source, image_ref.at[place_of(chip)], relay_send.at[i], relay_recv.at[i], at.other_core())

    at.each_chip(lambda i, chip, back: gather_copy(i, chip).start(), far_first=True)
    relay_copy(0, chunk_done, at.chip).start()
    image_ref[place_of(at.chip)] = chunk_done[...]

    def pass_on(i, chip, back):
        gather_copy(i, chip).wait_recv()
        relay_copy(i, image_ref.at[place_of(back)], back).start()

    at.each_chip(pass_on)
    loop(0, chips, lambda i: relay_copy(i, chunk_done, at.chip).wait())

    image = image_ref[...].reshape(NX, RANK)
    system_ref[:, :RANK] = gram(image, image)
    system_ref[:, RANK:] = gram(image, field_ref[...].reshape(NX, RANK))

    loop(1, fib_size, lambda i: tile_copy(i, at.fib).wait_send())
    loop(1, chips, lambda i: chunk_copy(i, at.chip).wait_send())
    loop(1, planes, lambda i: plane_copy(i).wait_send())
    loop(1, chips, lambda i: gather_copy(i, at.chip).wait_send())
    for distance in range(1, WINDOW):
        for copy in shift_copies(distance):
            copy.wait_send()


def normal_system(nodes, interp, table, order, basis, fib_size, pln_size):
    chips = fib_size // 2
    size = PIECES // 2 // chips
    vmem = lambda *shape: pltpu.VMEM(shape, jnp.float32)
    dma = lambda *n: pltpu.SemaphoreType.DMA(n)
    whole = pl.BlockSpec(memory_space=pltpu.VMEM)
    away = pl.BlockSpec(memory_space=pl.ANY)
    return pl.pallas_call(
        functools.partial(step_kernel, fib_size, pln_size),
        out_shape=jax.ShapeDtypeStruct((RANK, 2 * RANK), jnp.float32),
        in_specs=[away, away, pl.BlockSpec(memory_space=pltpu.SMEM), whole, away],
        out_specs=whole,
        scratch_shapes=[
            vmem(*nodes.shape), vmem(*interp.shape), vmem(*basis.shape),
            vmem(WINDOW - 1, CAP, 4 * RANK), vmem(WINDOW, CAP, 4 * RANK), vmem(PIECES, 4, RANK),
            vmem(PIECES, 4, RANK), vmem(PIECES, 4, RANK),
            vmem(PIECES, 4, RANK), vmem(size * chips, 4, RANK), vmem(size * chips, 4, RANK),
            vmem(chips, size, 4, RANK), vmem(size, 4, RANK), vmem(pln_size, size, 4, RANK),
            vmem(size, 4, RANK),
            dma(3), dma(WINDOW - 1, CUTS), dma(WINDOW - 1, CUTS), dma(fib_size), dma(fib_size),
            dma(2), dma(chips), dma(chips), dma(pln_size), dma(pln_size), dma(chips), dma(chips),
            dma(chips), dma(chips),
        ],
        compiler_params=pltpu.CompilerParams(collective_id=0, has_side_effects=True),
    )(nodes, interp, table, order, basis)


def per_device(nodal_values, interp_matrix, count_table, slot_order, start_basis):
    system = normal_system(
        nodal_values[0, 0], interp_matrix, jnp.transpose(count_table, (2, 0, 1)), slot_order[0], start_basis,
        lax.axis_size("fib"), lax.axis_size("pln"))
    return eliminate(system)[None, None]


def solution(mesh):
    placed = (P("pln", "fib", None, None), P(), P("pln", None, None), P("pln", "fib", None), P())
    return jax.shard_map(
        per_device,
        mesh=mesh,
        in_specs=placed,
        out_specs=P("pln", "fib", None, None),
        check_vma=False,
    )
```

```python
import functools

import jax
import jax.numpy as jnp
from jax import lax
from jax.experimental import pallas as pl
from jax.experimental.pallas import tpu as pltpu
from jax.sharding import PartitionSpec as P

NX = 768
RANK = 128
WINDOW = 3
CAP = 96
R_ELEM = 192
PIECES = NX // 4
X_CHIPS = 4
CUTS = 4
PIVOTS = 8
HIGHEST = lax.Precision.HIGHEST
MESH_ID = pl.DeviceIdType.MESH


def eliminate_kernel(system_ref, out_ref):
    blocks = RANK // 8
    left = [system_ref[8 * m:8 * m + 8, :RANK] for m in range(blocks)]
    right = [system_ref[8 * m:8 * m + 8, RANK:] for m in range(blocks)]
    rows = lax.broadcasted_iota(jnp.int32, (8, RANK), 0)

    def spread(row):
        return jnp.broadcast_to(row, (8, RANK))

    for k in range(0, RANK, PIVOTS):
        i, r = divmod(k, 8)
        row_left = [spread(left[i][r + a:r + a + 1, :]) for a in range(PIVOTS)]
        row_right = [spread(right[i][r + a:r + a + 1, :]) for a in range(PIVOTS)]
        corner = [[spread(row_left[a][:, k + b:k + b + 1]) if b >= a else None for b in range(PIVOTS)]
                  for a in range(PIVOTS)]
        ratio = [[None] * PIVOTS for _ in range(PIVOTS)]
        inverse = []
        for a in range(PIVOTS):
            inverse.append(1.0 / corner[a][a])
            for b in range(a + 1, PIVOTS):
                ratio[a][b] = corner[a][b] * inverse[a]
                for c in range(b, PIVOTS):
                    corner[b][c] = corner[b][c] - ratio[a][b] * corner[a][c]
                row_left[b] = row_left[b] - ratio[a][b] * row_left[a]
                row_right[b] = row_right[b] - ratio[a][b] * row_right[a]
        for a in range(PIVOTS):
            out_ref[k + a:k + a + 1, :] = (row_right[a] * lax.rsqrt(corner[a][a]))[:1]
        scaled_left = [row_left[a] * inverse[a] for a in range(PIVOTS)]
        scaled_right = [row_right[a] * inverse[a] for a in range(PIVOTS)]
        for m in range(i if r + PIVOTS < 8 else i + 1, blocks):
            factor = []
            for a in range(PIVOTS):
                column = spread(left[m][:, k + a:k + a + 1])
                if m == i:
                    column = jnp.where(rows >= r + PIVOTS, column, 0.0)
                for b in range(a):
                    column = column - ratio[b][a] * factor[b]
                factor.append(column)
            for a in range(PIVOTS):
                left[m] = left[m] - factor[a] * scaled_left[a]
                right[m] = right[m] - factor[a] * scaled_right[a]


def eliminate(system):
    return pl.pallas_call(
        eliminate_kernel,
        out_shape=jax.ShapeDtypeStruct((RANK, system.shape[1] - RANK), jnp.float32),
        in_specs=[pl.BlockSpec(memory_space=pltpu.VMEM)],
        out_specs=pl.BlockSpec(memory_space=pltpu.VMEM),
    )(system)


def remote(src, dst, send_sem, recv_sem, device):
    return pltpu.make_async_remote_copy(
        src_ref=src, dst_ref=dst, send_sem=send_sem, recv_sem=recv_sem,
        device_id=device, device_id_type=MESH_ID,
    )


def loop(low, high, body):
    def step(i, carry):
        body(i)
        return carry
    lax.fori_loop(low, high, step, 0)


class Place:
    def __init__(self, fib_size, pln_size):
        self.fib_size = fib_size
        self.chips = fib_size // 2
        self.depth = self.chips // X_CHIPS
        self.planes = pln_size
        self.fib = lax.axis_index("fib")
        self.pln = lax.axis_index("pln")
        self.core = lax.rem(self.fib, 2)
        self.chip = lax.div(self.fib, 2)
        self.z = lax.div(self.chip, X_CHIPS)
        self.x = lax.rem(self.chip, X_CHIPS)
        self.x_after = [lax.rem(self.x + step, X_CHIPS) for step in range(X_CHIPS)]
        self.x_before = [lax.rem(self.x + X_CHIPS - step, X_CHIPS) for step in range(X_CHIPS)]

    def at_fib(self, fib):
        return {"fib": fib, "pln": self.pln}

    def on_chip(self, chip):
        return self.at_fib(chip * 2 + self.core)

    def other_core(self):
        return self.at_fib(self.chip * 2 + 1 - self.core)

    def after(self, distance):
        return lax.rem(self.fib + distance, self.fib_size)

    def in_plane(self, step):
        return {"fib": self.fib, "pln": lax.rem(self.pln + step, self.planes)}

    def over_depth(self, row, far_first):
        if far_first:
            skip = (self.depth // 2 - 2) % (self.depth - 1)
            loop(0, self.depth - 1, lambda n: row(lax.rem(n + skip, self.depth - 1) + 1, True))
            row(0, False)
        else:
            row(0, False)
            loop(1, self.depth, lambda n: row(n, True))

    def each_chip(self, body, far_first=False):
        def row(z_step, with_own):
            ahead = lax.rem(self.z + z_step, self.depth) * X_CHIPS
            behind = lax.rem(self.z + self.depth - z_step, self.depth) * X_CHIPS
            for x_step in range(0 if with_own else 1, X_CHIPS):
                body(z_step * X_CHIPS + x_step, ahead + self.x_after[x_step], behind + self.x_before[x_step])
        self.over_depth(row, far_first)

    def each_device(self, body, far_first=False):
        def row(z_step, with_own):
            ahead = lax.rem(self.z + z_step, self.depth) * X_CHIPS
            for x_step in range(X_CHIPS):
                for turn in range(2):
                    if with_own or x_step or turn:
                        core = self.core if turn == 0 else 1 - self.core
                        body((z_step * X_CHIPS + x_step) * 2 + turn, (ahead + self.x_after[x_step]) * 2 + core)
        self.over_depth(row, far_first)


def pair(value):
    high = value.astype(jnp.bfloat16)
    return high, (value - high.astype(jnp.float32)).astype(jnp.bfloat16)


def mult(left, right):
    return jnp.dot(left, right, preferred_element_type=jnp.float32)


def gram(left, right):
    return lax.dot_general(left, right, (((0,), (0,)), ((), ())), precision=HIGHEST,
                           preferred_element_type=jnp.float32)


def step_kernel(fib_size, pln_size, nodes_hbm, interp_hbm, table_ref, order_ref, basis_hbm, system_ref,
                nodes_ref, interp_ref, basis_ref, outgoing, incoming, brick, field_ref, image_ref, part, other,
                half, chip_parts, chunk_sum, plane_parts, chunk_done, load_sems, shift_send, shift_recv,
                tile_send, tile_recv, core_sems, chip_send, chip_recv, plane_send, plane_recv, gather_send,
                gather_recv, relay_send, relay_recv):
    at = Place(fib_size, pln_size)
    chips, planes = at.chips, at.planes
    size = PIECES // 2 // chips
    split = size * chips
    run = PIECES // fib_size
    barrier = pltpu.get_barrier_semaphore()
    loads = [pltpu.make_async_copy(nodes_hbm, nodes_ref, load_sems.at[0]),
             pltpu.make_async_copy(interp_hbm, interp_ref, load_sems.at[1]),
             pltpu.make_async_copy(basis_hbm, basis_ref, load_sems.at[2])]

    def greet(device):
        pl.semaphore_signal(barrier, inc=1, device_id=device, device_id_type=MESH_ID)

    at.each_device(lambda i, fib: greet(at.at_fib(fib)), far_first=True)
    loop(1, planes, lambda i: greet(at.in_plane(i)))
    for load in loads:
        load.start()

    starts = [0]
    for distance in range(WINDOW - 1):
        starts.append(starts[-1] + table_ref[distance, 0, at.after(distance)])
    slots = (lax.broadcasted_iota(jnp.int32, (CAP, WINDOW * CAP), 1)
             - lax.broadcasted_iota(jnp.int32, (CAP, WINDOW * CAP), 0))
    for load in loads:
        load.wait()
    interp_high, interp_low = pair(interp_ref[...])
    nodes_high, nodes_low = pair(nodes_ref[...])

    def shift_copies(distance):
        rows = CAP // CUTS
        return [remote(outgoing.at[distance - 1, pl.ds(cut * rows, rows)],
                       incoming.at[distance, pl.ds(cut * rows, rows)],
                       shift_send.at[distance - 1, cut], shift_recv.at[distance - 1, cut],
                       at.at_fib(at.after(distance))) for cut in range(CUTS)]

    for distance in range(WINDOW - 1, -1, -1):
        if distance == 0:
            high, low = nodes_high[:CAP], nodes_low[:CAP]
        else:
            window = jnp.where(slots == starts[distance], 1.0, 0.0).astype(jnp.bfloat16)
            high = mult(window, nodes_high).astype(jnp.bfloat16)
            low = mult(window, nodes_low).astype(jnp.bfloat16)
        values = mult(high, interp_high) + (mult(high, interp_low) + mult(low, interp_high))
        if distance == 0:
            incoming[0] = values
        else:
            outgoing[distance - 1] = values
            if distance == WINDOW - 1:
                pl.semaphore_wait(barrier, fib_size + planes - 2)
            for copy in shift_copies(distance):
                copy.start()

    taken_near = table_ref[1, 0, at.fib]
    taken_far = table_ref[2, 0, at.fib]
    ranks = lax.broadcasted_iota(jnp.int32, (1, R_ELEM), 1)
    source = jnp.where(ranks < taken_far, 2 * CAP + ranks,
                       jnp.where(ranks < taken_far + taken_near, CAP + ranks - taken_far,
                                 ranks - taken_far - taken_near))
    places = lax.broadcasted_iota(jnp.int32, (R_ELEM, R_ELEM), 0)
    chosen = jnp.where(order_ref[...] == places, source.astype(jnp.float32), 0.0)
    chosen = jnp.sum(chosen, axis=1, keepdims=True).astype(jnp.int32)
    select = lax.broadcasted_iota(jnp.int32, (R_ELEM, WINDOW * CAP), 1) == chosen
    select = jnp.where(select, 1.0, 0.0).astype(jnp.bfloat16)
    for distance in range(WINDOW - 1, 0, -1):
        for copy in shift_copies(distance):
            copy.wait_recv()
    rows = incoming[...].reshape(WINDOW * CAP, 4 * RANK)
    high, low = pair(rows)
    rest = (rows - high.astype(jnp.float32)) - low.astype(jnp.float32)
    values = mult(select, high) + (mult(select, low) + mult(select, rest.astype(jnp.bfloat16)))
    for l in range(4):
        brick[:, l, :] = values[:, l * RANK:(l + 1) * RANK]

    def own_pieces(fib):
        return pl.ds(fib * run, run)

    def tile_copy(i, peer):
        return remote(brick.at[own_pieces(peer)], field_ref.at[own_pieces(at.fib)], tile_send.at[i],
                      tile_recv.at[i], at.at_fib(peer))

    at.each_device(lambda i, peer: tile_copy(i, peer).start(), far_first=True)
    field_ref[own_pieces(at.fib)] = brick[own_pieces(at.fib)]
    loop(1, fib_size, lambda i: tile_copy(i, at.fib).wait_recv())

    field = field_ref[...].reshape(NX, RANK)
    product = jnp.dot(field, gram(field, basis_ref[...]), precision=HIGHEST,
                      preferred_element_type=jnp.float32)
    part[...] = product.reshape(PIECES, 4, RANK)

    swap = remote(part.at[pl.ds((1 - at.core) * split, split)], other, core_sems.at[0], core_sems.at[1],
                  at.other_core())
    swap.start()
    swap.wait()
    half[...] = part[pl.ds(at.core * split, split)] + other[...]

    def chunk_copy(i, chip):
        return remote(half.at[pl.ds(chip * size, size)], chip_parts.at[i], chip_send.at[i], chip_recv.at[i],
                      at.on_chip(chip))

    at.each_chip(lambda i, chip, back: chunk_copy(i, chip).start(), far_first=True)
    chunk_sum[...] = half[pl.ds(at.chip * size, size)]

    def add_chunk(i):
        chunk_copy(i, at.chip).wait_recv()
        chunk_sum[...] += chip_parts[i]

    loop(1, chips, add_chunk)

    def plane_copy(i):
        return remote(chunk_sum, plane_parts.at[i], plane_send.at[i], plane_recv.at[i], at.in_plane(i))

    loop(1, planes, lambda i: plane_copy(i).start())
    chunk_done[...] = chunk_sum[...]

    def add_plane(i):
        plane_copy(i).wait_recv()
        chunk_done[...] += plane_parts[i]

    loop(1, planes, add_plane)

    def place_of(chip):
        return pl.ds(at.core * split + chip * size, size)

    def gather_copy(i, chip):
        return remote(chunk_done, image_ref.at[place_of(at.chip)], gather_send.at[i], gather_recv.at[i],
                      at.on_chip(chip))

    def relay_copy(i, source, chip):
        return remote(source, image_ref.at[place_of(chip)], relay_send.at[i], relay_recv.at[i], at.other_core())

    at.each_chip(lambda i, chip, back: gather_copy(i, chip).start(), far_first=True)
    relay_copy(0, chunk_done, at.chip).start()
    image_ref[place_of(at.chip)] = chunk_done[...]

    def pass_on(i, chip, back):
        gather_copy(i, chip).wait_recv()
        relay_copy(i, image_ref.at[place_of(back)], back).start()

    at.each_chip(pass_on)
    loop(0, chips, lambda i: relay_copy(i, chunk_done, at.chip).wait())

    image = image_ref[...].reshape(NX, RANK)
    system_ref[:, :RANK] = gram(image, image)
    system_ref[:, RANK:] = gram(image, field_ref[...].reshape(NX, RANK))

    loop(1, fib_size, lambda i: tile_copy(i, at.fib).wait_send())
    loop(1, chips, lambda i: chunk_copy(i, at.chip).wait_send())
    loop(1, planes, lambda i: plane_copy(i).wait_send())
    loop(1, chips, lambda i: gather_copy(i, at.chip).wait_send())
    for distance in range(1, WINDOW):
        for copy in shift_copies(distance):
            copy.wait_send()


def normal_system(nodes, interp, table, order, basis, fib_size, pln_size):
    chips = fib_size // 2
    size = PIECES // 2 // chips
    vmem = lambda *shape: pltpu.VMEM(shape, jnp.float32)
    dma = lambda *n: pltpu.SemaphoreType.DMA(n)
    whole = pl.BlockSpec(memory_space=pltpu.VMEM)
    away = pl.BlockSpec(memory_space=pl.ANY)
    return pl.pallas_call(
        functools.partial(step_kernel, fib_size, pln_size),
        out_shape=jax.ShapeDtypeStruct((RANK, 2 * RANK), jnp.float32),
        in_specs=[away, away, pl.BlockSpec(memory_space=pltpu.SMEM), whole, away],
        out_specs=whole,
        scratch_shapes=[
            vmem(*nodes.shape), vmem(*interp.shape), vmem(*basis.shape),
            vmem(WINDOW - 1, CAP, 4 * RANK), vmem(WINDOW, CAP, 4 * RANK), vmem(PIECES, 4, RANK),
            vmem(PIECES, 4, RANK), vmem(PIECES, 4, RANK),
            vmem(PIECES, 4, RANK), vmem(size * chips, 4, RANK), vmem(size * chips, 4, RANK),
            vmem(chips, size, 4, RANK), vmem(size, 4, RANK), vmem(pln_size, size, 4, RANK),
            vmem(size, 4, RANK),
            dma(3), dma(WINDOW - 1, CUTS), dma(WINDOW - 1, CUTS), dma(fib_size), dma(fib_size),
            dma(2), dma(chips), dma(chips), dma(pln_size), dma(pln_size), dma(chips), dma(chips),
            dma(chips), dma(chips),
        ],
        compiler_params=pltpu.CompilerParams(collective_id=0, has_side_effects=True),
    )(nodes, interp, table, order, basis)


def per_device(nodal_values, interp_matrix, count_table, slot_order, start_basis):
    system = normal_system(
        nodal_values[0, 0], interp_matrix, jnp.transpose(count_table, (2, 0, 1)), slot_order[0], start_basis,
        lax.axis_size("fib"), lax.axis_size("pln"))
    return eliminate(system)[None, None]


def solution(mesh):
    placed = (P("pln", "fib", None, None), P(), P("pln", None, None), P("pln", "fib", None), P())
    return jax.shard_map(
        per_device,
        mesh=mesh,
        in_specs=placed,
        out_specs=P("pln", "fib", None, None),
        check_vma=False,
    )
```

```python
import functools

import jax
import jax.numpy as jnp
from jax import lax
from jax.experimental import pallas as pl
from jax.experimental.pallas import tpu as pltpu
from jax.sharding import PartitionSpec as P

NX = 768
RANK = 128
WINDOW = 3
CAP = 96
R_ELEM = 192
PIECES = NX // 4
X_CHIPS = 4
CUTS = 4
PIVOTS = 8
HIGHEST = lax.Precision.HIGHEST
MESH_ID = pl.DeviceIdType.MESH


def eliminate_kernel(system_ref, out_ref):
    blocks = RANK // 8
    left = [system_ref[8 * m:8 * m + 8, :RANK] for m in range(blocks)]
    right = [system_ref[8 * m:8 * m + 8, RANK:] for m in range(blocks)]
    rows = lax.broadcasted_iota(jnp.int32, (8, RANK), 0)

    def spread(row):
        return jnp.broadcast_to(row, (8, RANK))

    for k in range(0, RANK, PIVOTS):
        i, r = divmod(k, 8)
        row_left = [spread(left[i][r + a:r + a + 1, :]) for a in range(PIVOTS)]
        row_right = [spread(right[i][r + a:r + a + 1, :]) for a in range(PIVOTS)]
        corner = [[spread(row_left[a][:, k + b:k + b + 1]) if b >= a else None for b in range(PIVOTS)]
                  for a in range(PIVOTS)]
        ratio = [[None] * PIVOTS for _ in range(PIVOTS)]
        inverse = []
        for a in range(PIVOTS):
            inverse.append(1.0 / corner[a][a])
            for b in range(a + 1, PIVOTS):
                ratio[a][b] = corner[a][b] * inverse[a]
                for c in range(b, PIVOTS):
                    corner[b][c] = corner[b][c] - ratio[a][b] * corner[a][c]
                row_left[b] = row_left[b] - ratio[a][b] * row_left[a]
                row_right[b] = row_right[b] - ratio[a][b] * row_right[a]
        for a in range(PIVOTS):
            out_ref[k + a:k + a + 1, :] = (row_right[a] * lax.rsqrt(corner[a][a]))[:1]
        scaled_left = [row_left[a] * inverse[a] for a in range(PIVOTS)]
        scaled_right = [row_right[a] * inverse[a] for a in range(PIVOTS)]
        for m in range(i if r + PIVOTS < 8 else i + 1, blocks):
            factor = []
            for a in range(PIVOTS):
                column = spread(left[m][:, k + a:k + a + 1])
                if m == i:
                    column = jnp.where(rows >= r + PIVOTS, column, 0.0)
                for b in range(a):
                    column = column - ratio[b][a] * factor[b]
                factor.append(column)
            for a in range(PIVOTS):
                left[m] = left[m] - factor[a] * scaled_left[a]
                right[m] = right[m] - factor[a] * scaled_right[a]


def eliminate(system):
    return pl.pallas_call(
        eliminate_kernel,
        out_shape=jax.ShapeDtypeStruct((RANK, system.shape[1] - RANK), jnp.float32),
        in_specs=[pl.BlockSpec(memory_space=pltpu.VMEM)],
        out_specs=pl.BlockSpec(memory_space=pltpu.VMEM),
    )(system)


def remote(src, dst, send_sem, recv_sem, device):
    return pltpu.make_async_remote_copy(
        src_ref=src, dst_ref=dst, send_sem=send_sem, recv_sem=recv_sem,
        device_id=device, device_id_type=MESH_ID,
    )


def loop(low, high, body):
    def step(i, carry):
        body(i)
        return carry
    lax.fori_loop(low, high, step, 0)


class Place:
    def __init__(self, fib_size, pln_size):
        self.fib_size = fib_size
        self.chips = fib_size // 2
        self.depth = self.chips // X_CHIPS
        self.planes = pln_size
        self.fib = lax.axis_index("fib")
        self.pln = lax.axis_index("pln")
        self.core = lax.rem(self.fib, 2)
        self.chip = lax.div(self.fib, 2)
        self.z = lax.div(self.chip, X_CHIPS)
        self.x = lax.rem(self.chip, X_CHIPS)
        self.x_after = [lax.rem(self.x + step, X_CHIPS) for step in range(X_CHIPS)]
        self.x_before = [lax.rem(self.x + X_CHIPS - step, X_CHIPS) for step in range(X_CHIPS)]

    def at_fib(self, fib):
        return {"fib": fib, "pln": self.pln}

    def on_chip(self, chip):
        return self.at_fib(chip * 2 + self.core)

    def other_core(self):
        return self.at_fib(self.chip * 2 + 1 - self.core)

    def along_z(self, step):
        return self.on_chip(lax.rem(self.z + step, self.depth) * X_CHIPS + self.x)

    def along_x(self, step):
        return self.on_chip(self.z * X_CHIPS + self.x_after[step])

    def after(self, distance):
        return lax.rem(self.fib + distance, self.fib_size)

    def in_plane(self, step):
        return {"fib": self.fib, "pln": lax.rem(self.pln + step, self.planes)}

    def over_depth(self, row, far_first):
        if far_first:
            skip = (self.depth // 2 - 2) % (self.depth - 1)
            loop(0, self.depth - 1, lambda n: row(lax.rem(n + skip, self.depth - 1) + 1, True))
            row(0, False)
        else:
            row(0, False)
            loop(1, self.depth, lambda n: row(n, True))

    def each_chip(self, body, far_first=False):
        def row(z_step, with_own):
            ahead = lax.rem(self.z + z_step, self.depth) * X_CHIPS
            behind = lax.rem(self.z + self.depth - z_step, self.depth) * X_CHIPS
            for x_step in range(0 if with_own else 1, X_CHIPS):
                body(z_step * X_CHIPS + x_step, ahead + self.x_after[x_step], behind + self.x_before[x_step])
        self.over_depth(row, far_first)

    def each_device(self, body, far_first=False):
        def row(z_step, with_own):
            ahead = lax.rem(self.z + z_step, self.depth) * X_CHIPS
            for x_step in range(X_CHIPS):
                for turn in range(2):
                    if with_own or x_step or turn:
                        core = self.core if turn == 0 else 1 - self.core
                        body((z_step * X_CHIPS + x_step) * 2 + turn, (ahead + self.x_after[x_step]) * 2 + core)
        self.over_depth(row, far_first)


def pair(value):
    high = value.astype(jnp.bfloat16)
    return high, (value - high.astype(jnp.float32)).astype(jnp.bfloat16)


def mult(left, right):
    return jnp.dot(left, right, preferred_element_type=jnp.float32)


def gram(left, right):
    return lax.dot_general(left, right, (((0,), (0,)), ((), ())), precision=HIGHEST,
                           preferred_element_type=jnp.float32)


def step_kernel(fib_size, pln_size, nodes_hbm, interp_hbm, table_ref, order_ref, basis_hbm, system_ref,
                nodes_ref, interp_ref, basis_ref, outgoing, incoming, brick, field_ref, image_ref, part, other,
                half, chip_parts, chunk_sum, plane_parts, chunk_done, load_sems, shift_send, shift_recv,
                tile_send, tile_recv, core_sems, chip_send, chip_recv, plane_send, plane_recv, gather_send,
                gather_recv, relay_send, relay_recv, ready):
    at = Place(fib_size, pln_size)
    chips, planes = at.chips, at.planes
    size = PIECES // 2 // chips
    split = size * chips
    run = PIECES // fib_size
    barrier = pltpu.get_barrier_semaphore()
    loads = [pltpu.make_async_copy(nodes_hbm, nodes_ref, load_sems.at[0]),
             pltpu.make_async_copy(interp_hbm, interp_ref, load_sems.at[1]),
             pltpu.make_async_copy(basis_hbm, basis_ref, load_sems.at[2])]

    def greet(device):
        pl.semaphore_signal(barrier, inc=1, device_id=device, device_id_type=MESH_ID)

    near = [at.along_z(1), at.along_z(at.depth - 1)], [at.along_x(1), at.along_x(X_CHIPS - 1)], [at.other_core()]
    layers = [at.in_plane(1), at.in_plane(planes - 1)]
    window = [at.at_fib(at.after(step)) for step in (1, 2, fib_size - 1, fib_size - 2)]
    first = near[0] + near[1] + near[2] + layers + window
    for device in first:
        greet(device)
    for load in loads:
        load.start()

    starts = [0]
    for distance in range(WINDOW - 1):
        starts.append(starts[-1] + table_ref[distance, 0, at.after(distance)])
    slots = (lax.broadcasted_iota(jnp.int32, (CAP, WINDOW * CAP), 1)
             - lax.broadcasted_iota(jnp.int32, (CAP, WINDOW * CAP), 0))
    for load in loads:
        load.wait()
    interp_high, interp_low = pair(interp_ref[...])
    nodes_high, nodes_low = pair(nodes_ref[...])

    def shift_copies(distance):
        rows = CAP // CUTS
        return [remote(outgoing.at[distance - 1, pl.ds(cut * rows, rows)],
                       incoming.at[distance, pl.ds(cut * rows, rows)],
                       shift_send.at[distance - 1, cut], shift_recv.at[distance - 1, cut],
                       at.at_fib(at.after(distance))) for cut in range(CUTS)]

    for distance in range(WINDOW - 1, -1, -1):
        if distance == 0:
            high, low = nodes_high[:CAP], nodes_low[:CAP]
        else:
            window = jnp.where(slots == starts[distance], 1.0, 0.0).astype(jnp.bfloat16)
            high = mult(window, nodes_high).astype(jnp.bfloat16)
            low = mult(window, nodes_low).astype(jnp.bfloat16)
        values = mult(high, interp_high) + (mult(high, interp_low) + mult(low, interp_high))
        if distance == 0:
            incoming[0] = values
        else:
            outgoing[distance - 1] = values
            if distance == WINDOW - 1:
                pl.semaphore_wait(barrier, len(first))
            for copy in shift_copies(distance):
                copy.start()

    taken_near = table_ref[1, 0, at.fib]
    taken_far = table_ref[2, 0, at.fib]
    ranks = lax.broadcasted_iota(jnp.int32, (1, R_ELEM), 1)
    source = jnp.where(ranks < taken_far, 2 * CAP + ranks,
                       jnp.where(ranks < taken_far + taken_near, CAP + ranks - taken_far,
                                 ranks - taken_far - taken_near))
    places = lax.broadcasted_iota(jnp.int32, (R_ELEM, R_ELEM), 0)
    chosen = jnp.where(order_ref[...] == places, source.astype(jnp.float32), 0.0)
    chosen = jnp.sum(chosen, axis=1, keepdims=True).astype(jnp.int32)
    select = lax.broadcasted_iota(jnp.int32, (R_ELEM, WINDOW * CAP), 1) == chosen
    select = jnp.where(select, 1.0, 0.0).astype(jnp.bfloat16)

    rounds = [near[0]] * (at.depth // 2) + [near[1]] * (X_CHIPS // 2) + [near[2]]
    for turn, devices in enumerate(rounds):
        pairs = [(turn, devices)]
        if turn < planes // 2:
            pairs.append((len(rounds) + turn, layers))
        for slot, others in pairs:
            for device in others:
                pl.semaphore_signal(ready.at[slot], inc=1, device_id=device, device_id_type=MESH_ID)
        for slot, others in pairs:
            pl.semaphore_wait(ready.at[slot], len(others))

    for distance in range(WINDOW - 1, 0, -1):
        for copy in shift_copies(distance):
            copy.wait_recv()
    rows = incoming[...].reshape(WINDOW * CAP, 4 * RANK)
    high, low = pair(rows)
    rest = (rows - high.astype(jnp.float32)) - low.astype(jnp.float32)
    values = mult(select, high) + (mult(select, low) + mult(select, rest.astype(jnp.bfloat16)))
    for l in range(4):
        brick[:, l, :] = values[:, l * RANK:(l + 1) * RANK]

    def own_pieces(fib):
        return pl.ds(fib * run, run)

    def tile_copy(i, peer):
        return remote(brick.at[own_pieces(peer)], field_ref.at[own_pieces(at.fib)], tile_send.at[i],
                      tile_recv.at[i], at.at_fib(peer))

    at.each_device(lambda i, peer: tile_copy(i, peer).start(), far_first=True)
    field_ref[own_pieces(at.fib)] = brick[own_pieces(at.fib)]
    loop(1, fib_size, lambda i: tile_copy(i, at.fib).wait_recv())

    coefficients = gram(field_ref[...].reshape(NX, RANK), basis_ref[...])

    def partial_image(core):
        rows = field_ref[pl.ds(core * split, split)].reshape(NX // 2, RANK)
        product = jnp.dot(rows, coefficients, precision=HIGHEST, preferred_element_type=jnp.float32)
        return product.reshape(split, 4, RANK)

    part[...] = partial_image(1 - at.core)
    swap = remote(part, other, core_sems.at[0], core_sems.at[1], at.other_core())
    swap.start()
    half[...] = partial_image(at.core)
    swap.wait()
    half[...] += other[...]

    def chunk_copy(i, chip):
        return remote(half.at[pl.ds(chip * size, size)], chip_parts.at[i], chip_send.at[i], chip_recv.at[i],
                      at.on_chip(chip))

    at.each_chip(lambda i, chip, back: chunk_copy(i, chip).start(), far_first=True)
    chunk_sum[...] = half[pl.ds(at.chip * size, size)]

    def add_chunk(i):
        chunk_copy(i, at.chip).wait_recv()
        chunk_sum[...] += chip_parts[i]

    loop(1, chips, add_chunk)

    def plane_copy(i):
        return remote(chunk_sum, plane_parts.at[i], plane_send.at[i], plane_recv.at[i], at.in_plane(i))

    loop(1, planes, lambda i: plane_copy(i).start())
    chunk_done[...] = chunk_sum[...]

    def add_plane(i):
        plane_copy(i).wait_recv()
        chunk_done[...] += plane_parts[i]

    loop(1, planes, add_plane)

    def place_of(chip):
        return pl.ds(at.core * split + chip * size, size)

    def gather_copy(i, chip):
        return remote(chunk_done, image_ref.at[place_of(at.chip)], gather_send.at[i], gather_recv.at[i],
                      at.on_chip(chip))

    def relay_copy(i, source, chip):
        return remote(source, image_ref.at[place_of(chip)], relay_send.at[i], relay_recv.at[i], at.other_core())

    at.each_chip(lambda i, chip, back: gather_copy(i, chip).start(), far_first=True)
    relay_copy(0, chunk_done, at.chip).start()
    image_ref[place_of(at.chip)] = chunk_done[...]

    def pass_on(i, chip, back):
        gather_copy(i, chip).wait_recv()
        relay_copy(i, image_ref.at[place_of(back)], back).start()

    at.each_chip(pass_on)
    loop(0, chips, lambda i: relay_copy(i, chunk_done, at.chip).wait())

    image = image_ref[...].reshape(NX, RANK)
    system_ref[:, :RANK] = gram(image, image)
    system_ref[:, RANK:] = gram(image, field_ref[...].reshape(NX, RANK))

    loop(1, fib_size, lambda i: tile_copy(i, at.fib).wait_send())
    loop(1, chips, lambda i: chunk_copy(i, at.chip).wait_send())
    loop(1, planes, lambda i: plane_copy(i).wait_send())
    loop(1, chips, lambda i: gather_copy(i, at.chip).wait_send())
    for distance in range(1, WINDOW):
        for copy in shift_copies(distance):
            copy.wait_send()


def normal_system(nodes, interp, table, order, basis, fib_size, pln_size):
    chips = fib_size // 2
    size = PIECES // 2 // chips
    vmem = lambda *shape: pltpu.VMEM(shape, jnp.float32)
    dma = lambda *n: pltpu.SemaphoreType.DMA(n)
    whole = pl.BlockSpec(memory_space=pltpu.VMEM)
    away = pl.BlockSpec(memory_space=pl.ANY)
    return pl.pallas_call(
        functools.partial(step_kernel, fib_size, pln_size),
        out_shape=jax.ShapeDtypeStruct((RANK, 2 * RANK), jnp.float32),
        in_specs=[away, away, pl.BlockSpec(memory_space=pltpu.SMEM), whole, away],
        out_specs=whole,
        scratch_shapes=[
            vmem(*nodes.shape), vmem(*interp.shape), vmem(*basis.shape),
            vmem(WINDOW - 1, CAP, 4 * RANK), vmem(WINDOW, CAP, 4 * RANK), vmem(PIECES, 4, RANK),
            vmem(PIECES, 4, RANK), vmem(PIECES, 4, RANK),
            vmem(size * chips, 4, RANK), vmem(size * chips, 4, RANK), vmem(size * chips, 4, RANK),
            vmem(chips, size, 4, RANK), vmem(size, 4, RANK), vmem(pln_size, size, 4, RANK),
            vmem(size, 4, RANK),
            dma(3), dma(WINDOW - 1, CUTS), dma(WINDOW - 1, CUTS), dma(fib_size), dma(fib_size),
            dma(2), dma(chips), dma(chips), dma(pln_size), dma(pln_size), dma(chips), dma(chips),
            dma(chips), dma(chips),
            pltpu.SemaphoreType.REGULAR((fib_size // 2 // X_CHIPS // 2 + X_CHIPS // 2 + 1 + pln_size // 2,)),
        ],
        compiler_params=pltpu.CompilerParams(collective_id=0, has_side_effects=True),
    )(nodes, interp, table, order, basis)


def per_device(nodal_values, interp_matrix, count_table, slot_order, start_basis):
    system = normal_system(
        nodal_values[0, 0], interp_matrix, jnp.transpose(count_table, (2, 0, 1)), slot_order[0], start_basis,
        lax.axis_size("fib"), lax.axis_size("pln"))
    return eliminate(system)[None, None]


def solution(mesh):
    placed = (P("pln", "fib", None, None), P(), P("pln", None, None), P("pln", "fib", None), P())
    return jax.shard_map(
        per_device,
        mesh=mesh,
        in_specs=placed,
        out_specs=P("pln", "fib", None, None),
        check_vma=False,
    )
```

```python
import functools

import jax
import jax.numpy as jnp
from jax import lax
from jax.experimental import pallas as pl
from jax.experimental.pallas import tpu as pltpu
from jax.sharding import PartitionSpec as P

NX = 768
RANK = 128
WINDOW = 3
CAP = 96
R_ELEM = 192
PIECES = NX // 4
X_CHIPS = 4
CUTS = 4
PIVOTS = 8
HIGHEST = lax.Precision.HIGHEST
MESH_ID = pl.DeviceIdType.MESH


def eliminate_kernel(system_ref, out_ref):
    blocks = RANK // 8
    left = [system_ref[8 * m:8 * m + 8, :RANK] for m in range(blocks)]
    right = [system_ref[8 * m:8 * m + 8, RANK:] for m in range(blocks)]
    rows = lax.broadcasted_iota(jnp.int32, (8, RANK), 0)

    def spread(row):
        return jnp.broadcast_to(row, (8, RANK))

    for k in range(0, RANK, PIVOTS):
        i, r = divmod(k, 8)
        row_left = [spread(left[i][r + a:r + a + 1, :]) for a in range(PIVOTS)]
        row_right = [spread(right[i][r + a:r + a + 1, :]) for a in range(PIVOTS)]
        corner = [[spread(row_left[a][:, k + b:k + b + 1]) if b >= a else None for b in range(PIVOTS)]
                  for a in range(PIVOTS)]
        ratio = [[None] * PIVOTS for _ in range(PIVOTS)]
        inverse = []
        for a in range(PIVOTS):
            inverse.append(1.0 / corner[a][a])
            for b in range(a + 1, PIVOTS):
                ratio[a][b] = corner[a][b] * inverse[a]
                for c in range(b, PIVOTS):
                    corner[b][c] = corner[b][c] - ratio[a][b] * corner[a][c]
                row_left[b] = row_left[b] - ratio[a][b] * row_left[a]
                row_right[b] = row_right[b] - ratio[a][b] * row_right[a]
        for a in range(PIVOTS):
            out_ref[k + a:k + a + 1, :] = (row_right[a] * lax.rsqrt(corner[a][a]))[:1]
        scaled_left = [row_left[a] * inverse[a] for a in range(PIVOTS)]
        scaled_right = [row_right[a] * inverse[a] for a in range(PIVOTS)]
        for m in range(i if r + PIVOTS < 8 else i + 1, blocks):
            factor = []
            for a in range(PIVOTS):
                column = spread(left[m][:, k + a:k + a + 1])
                if m == i:
                    column = jnp.where(rows >= r + PIVOTS, column, 0.0)
                for b in range(a):
                    column = column - ratio[b][a] * factor[b]
                factor.append(column)
            for a in range(PIVOTS):
                left[m] = left[m] - factor[a] * scaled_left[a]
                right[m] = right[m] - factor[a] * scaled_right[a]


def eliminate(system):
    return pl.pallas_call(
        eliminate_kernel,
        out_shape=jax.ShapeDtypeStruct((RANK, system.shape[1] - RANK), jnp.float32),
        in_specs=[pl.BlockSpec(memory_space=pltpu.VMEM)],
        out_specs=pl.BlockSpec(memory_space=pltpu.VMEM),
    )(system)


def remote(src, dst, send_sem, recv_sem, device):
    return pltpu.make_async_remote_copy(
        src_ref=src, dst_ref=dst, send_sem=send_sem, recv_sem=recv_sem,
        device_id=device, device_id_type=MESH_ID,
    )


def loop(low, high, body):
    def step(i, carry):
        body(i)
        return carry
    lax.fori_loop(low, high, step, 0)


class Place:
    def __init__(self, fib_size, pln_size):
        self.fib_size = fib_size
        self.chips = fib_size // 2
        self.depth = self.chips // X_CHIPS
        self.planes = pln_size
        self.fib = lax.axis_index("fib")
        self.pln = lax.axis_index("pln")
        self.core = lax.rem(self.fib, 2)
        self.chip = lax.div(self.fib, 2)
        self.z = lax.div(self.chip, X_CHIPS)
        self.x = lax.rem(self.chip, X_CHIPS)
        self.x_after = [lax.rem(self.x + step, X_CHIPS) for step in range(X_CHIPS)]
        self.x_before = [lax.rem(self.x + X_CHIPS - step, X_CHIPS) for step in range(X_CHIPS)]

    def at_fib(self, fib):
        return {"fib": fib, "pln": self.pln}

    def on_chip(self, chip):
        return self.at_fib(chip * 2 + self.core)

    def other_core(self):
        return self.at_fib(self.chip * 2 + 1 - self.core)

    def along_z(self, step):
        return self.on_chip(lax.rem(self.z + step, self.depth) * X_CHIPS + self.x)

    def along_x(self, step):
        return self.on_chip(self.z * X_CHIPS + self.x_after[step])

    def after(self, distance):
        return lax.rem(self.fib + distance, self.fib_size)

    def in_plane(self, step):
        return {"fib": self.fib, "pln": lax.rem(self.pln + step, self.planes)}

    def over_depth(self, row, far_first):
        if far_first:
            skip = (self.depth // 2 - 2) % (self.depth - 1)
            loop(0, self.depth - 1, lambda n: row(lax.rem(n + skip, self.depth - 1) + 1, True))
            row(0, False)
        else:
            row(0, False)
            loop(1, self.depth, lambda n: row(n, True))

    def row_of_chips(self, body):
        def row(z_step, with_own=True):
            ahead = lax.rem(self.z + z_step, self.depth) * X_CHIPS
            behind = lax.rem(self.z + self.depth - z_step, self.depth) * X_CHIPS
            for x_step in range(0 if with_own else 1, X_CHIPS):
                body(z_step * X_CHIPS + x_step, ahead + self.x_after[x_step], behind + self.x_before[x_step])
        return row

    def each_chip(self, body, far_first=False):
        self.over_depth(self.row_of_chips(body), far_first)

    def each_device(self, body, far_first=False):
        def row(z_step, with_own):
            ahead = lax.rem(self.z + z_step, self.depth) * X_CHIPS
            for x_step in range(X_CHIPS):
                for turn in range(2):
                    if with_own or x_step or turn:
                        core = self.core if turn == 0 else 1 - self.core
                        body((z_step * X_CHIPS + x_step) * 2 + turn, (ahead + self.x_after[x_step]) * 2 + core)
        self.over_depth(row, far_first)


def pair(value):
    high = value.astype(jnp.bfloat16)
    return high, (value - high.astype(jnp.float32)).astype(jnp.bfloat16)


def mult(left, right):
    return jnp.dot(left, right, preferred_element_type=jnp.float32)


def mult3(left, right, contract=1):
    dims = (((contract,), (0,)), ((), ()))
    (left_high, left_low), (right_high, right_low) = pair(left), pair(right)

    def product(a, b):
        return lax.dot_general(a, b, dims, preferred_element_type=jnp.float32)

    return product(left_high, right_high) + (product(left_high, right_low) + product(left_low, right_high))


def gram(left, right):
    return lax.dot_general(left, right, (((0,), (0,)), ((), ())), precision=HIGHEST,
                           preferred_element_type=jnp.float32)


def step_kernel(fib_size, pln_size, nodes_hbm, interp_hbm, table_ref, order_ref, basis_hbm, system_ref,
                nodes_ref, interp_ref, basis_ref, outgoing, incoming, brick, field_ref, image_ref, part, other,
                half, chip_parts, chunk_sum, plane_parts, chunk_done, load_sems, shift_send, shift_recv,
                tile_send, tile_recv, core_sems, chip_send, chip_recv, plane_send, plane_recv, gather_send,
                gather_recv, relay_send, relay_recv, ready, direct_send, direct_recv):
    at = Place(fib_size, pln_size)
    chips, planes = at.chips, at.planes
    size = PIECES // 2 // chips
    split = size * chips
    run = PIECES // fib_size
    barrier = pltpu.get_barrier_semaphore()
    loads = [pltpu.make_async_copy(nodes_hbm, nodes_ref, load_sems.at[0]),
             pltpu.make_async_copy(interp_hbm, interp_ref, load_sems.at[1]),
             pltpu.make_async_copy(basis_hbm, basis_ref, load_sems.at[2])]

    def greet(device):
        pl.semaphore_signal(barrier, inc=1, device_id=device, device_id_type=MESH_ID)

    reach_z, reach_y = at.depth // 4, planes // 4
    near_z = [at.along_z(step) for n in range(reach_z, 0, -1) for step in (n, at.depth - n)]
    near_y = [at.in_plane(step) for n in range(reach_y, 0, -1) for step in (n, planes - n)]
    line_x = [at.along_x(step) for step in range(1, X_CHIPS)]
    window = [at.at_fib(at.after(step)) for step in (1, 2, fib_size - 1, fib_size - 2)]
    first = near_z + near_y + line_x + window + [at.other_core()]
    for device in first:
        greet(device)
    for load in loads:
        load.start()

    starts = [0]
    for distance in range(WINDOW - 1):
        starts.append(starts[-1] + table_ref[distance, 0, at.after(distance)])
    slots = (lax.broadcasted_iota(jnp.int32, (CAP, WINDOW * CAP), 1)
             - lax.broadcasted_iota(jnp.int32, (CAP, WINDOW * CAP), 0))
    for load in loads:
        load.wait()
    interp_high, interp_low = pair(interp_ref[...])
    nodes_high, nodes_low = pair(nodes_ref[...])

    def shift_copies(distance):
        rows = CAP // CUTS
        return [remote(outgoing.at[distance - 1, pl.ds(cut * rows, rows)],
                       incoming.at[distance, pl.ds(cut * rows, rows)],
                       shift_send.at[distance - 1, cut], shift_recv.at[distance - 1, cut],
                       at.at_fib(at.after(distance))) for cut in range(CUTS)]

    for distance in range(WINDOW - 1, -1, -1):
        if distance == 0:
            high, low = nodes_high[:CAP], nodes_low[:CAP]
        else:
            window = jnp.where(slots == starts[distance], 1.0, 0.0).astype(jnp.bfloat16)
            high = mult(window, nodes_high).astype(jnp.bfloat16)
            low = mult(window, nodes_low).astype(jnp.bfloat16)
        values = mult(high, interp_high) + (mult(high, interp_low) + mult(low, interp_high))
        if distance == 0:
            incoming[0] = values
        else:
            outgoing[distance - 1] = values
            if distance == WINDOW - 1:
                pl.semaphore_wait(barrier, len(first))
            for copy in shift_copies(distance):
                copy.start()

    taken_near = table_ref[1, 0, at.fib]
    taken_far = table_ref[2, 0, at.fib]
    ranks = lax.broadcasted_iota(jnp.int32, (1, R_ELEM), 1)
    source = jnp.where(ranks < taken_far, 2 * CAP + ranks,
                       jnp.where(ranks < taken_far + taken_near, CAP + ranks - taken_far,
                                 ranks - taken_far - taken_near))
    places = lax.broadcasted_iota(jnp.int32, (R_ELEM, R_ELEM), 0)
    chosen = jnp.where(order_ref[...] == places, source.astype(jnp.float32), 0.0)
    chosen = jnp.sum(chosen, axis=1, keepdims=True).astype(jnp.int32)
    select = lax.broadcasted_iota(jnp.int32, (R_ELEM, WINDOW * CAP), 1) == chosen
    select = jnp.where(select, 1.0, 0.0).astype(jnp.bfloat16)

    for pairs in (((0, near_z[:2]), (1, near_y[:2])), ((2, line_x),), ((3, [at.other_core()]),)):
        for slot, others in pairs:
            for device in others:
                pl.semaphore_signal(ready.at[slot], inc=1, device_id=device, device_id_type=MESH_ID)
        for slot, others in pairs:
            pl.semaphore_wait(ready.at[slot], len(others))

    for distance in range(WINDOW - 1, 0, -1):
        for copy in shift_copies(distance):
            copy.wait_recv()
    rows = incoming[...].reshape(WINDOW * CAP, 4 * RANK)
    high, low = pair(rows)
    rest = (rows - high.astype(jnp.float32)) - low.astype(jnp.float32)
    values = mult(select, high) + (mult(select, low) + mult(select, rest.astype(jnp.bfloat16)))
    for l in range(4):
        brick[:, l, :] = values[:, l * RANK:(l + 1) * RANK]

    def own_pieces(fib):
        return pl.ds(fib * run, run)

    def tile_copy(i, peer):
        return remote(brick.at[own_pieces(peer)], field_ref.at[own_pieces(at.fib)], tile_send.at[i],
                      tile_recv.at[i], at.at_fib(peer))

    at.each_device(lambda i, peer: tile_copy(i, peer).start(), far_first=True)
    field_ref[own_pieces(at.fib)] = brick[own_pieces(at.fib)]
    loop(1, fib_size, lambda i: tile_copy(i, at.fib).wait_recv())

    coefficients = mult3(field_ref[...].reshape(NX, RANK), basis_ref[...], 0)

    def partial_image(core):
        rows = field_ref[pl.ds(core * split, split)].reshape(NX // 2, RANK)
        return mult3(rows, coefficients).reshape(split, 4, RANK)

    part[...] = partial_image(1 - at.core)
    swap = remote(part, other, core_sems.at[0], core_sems.at[1], at.other_core())
    swap.start()
    half[...] = partial_image(at.core)
    swap.wait()
    half[...] += other[...]

    def chunk_copy(i, chip):
        return remote(half.at[pl.ds(chip * size, size)], chip_parts.at[i], chip_send.at[i], chip_recv.at[i],
                      at.on_chip(chip))

    at.each_chip(lambda i, chip, back: chunk_copy(i, chip).start(), far_first=True)
    chunk_sum[...] = half[pl.ds(at.chip * size, size)]

    def add_chunk(i):
        chunk_copy(i, at.chip).wait_recv()
        chunk_sum[...] += chip_parts[i]

    loop(1, chips, add_chunk)

    def plane_copy(i):
        return remote(chunk_sum, plane_parts.at[i], plane_send.at[i], plane_recv.at[i], at.in_plane(i))

    loop(1, planes, lambda i: plane_copy(i).start())
    chunk_done[...] = chunk_sum[...]

    def add_plane(i):
        plane_copy(i).wait_recv()
        chunk_done[...] += plane_parts[i]

    loop(1, planes, add_plane)

    def place_of(chip):
        return pl.ds(at.core * split + chip * size, size)

    def gather_copy(i, chip):
        return remote(chunk_done, image_ref.at[place_of(at.chip)], gather_send.at[i], gather_recv.at[i],
                      at.on_chip(chip))

    def relay_copy(i, source, chip):
        return remote(source, image_ref.at[place_of(chip)], relay_send.at[i], relay_recv.at[i], at.other_core())

    far = at.depth // 2

    def direct_copy(i, chip):
        return remote(chunk_done, image_ref.at[place_of(at.chip)], direct_send.at[i], direct_recv.at[i],
                      at.at_fib(chip * 2 + 1 - at.core))

    def send_far(i, chip, back):
        gather_copy(i, chip).start()
        direct_copy(i - far * X_CHIPS, chip).start()

    def other_rows(row):
        loop(far + 1, at.depth, row)
        loop(1, far, row)
        row(0, False)

    at.row_of_chips(send_far)(far)
    other_rows(at.row_of_chips(lambda i, chip, back: gather_copy(i, chip).start()))
    relay_copy(0, chunk_done, at.chip).start()
    image_ref[place_of(at.chip)] = chunk_done[...]

    def pass_on(i, chip, back):
        gather_copy(i, chip).wait_recv()
        relay_copy(i, image_ref.at[place_of(back)], back).start()

    row = at.row_of_chips(pass_on)
    row(0, False)
    loop(1, far, row)
    loop(far + 1, at.depth, row)
    loop(far * X_CHIPS, (far + 1) * X_CHIPS, lambda i: gather_copy(i, at.chip).wait_recv())

    def half_system(core):
        image = image_ref[pl.ds(core * split, split)].reshape(NX // 2, RANK)
        field = field_ref[pl.ds(core * split, split)].reshape(NX // 2, RANK)
        return gram(image, image), mult3(image, field, 0)

    own_normal, own_right = half_system(at.core)
    for low, high in ((0, far * X_CHIPS), ((far + 1) * X_CHIPS, chips)):
        loop(low, high, lambda i: relay_copy(i, chunk_done, at.chip).wait())
    loop(0, X_CHIPS, lambda i: direct_copy(i, at.chip).wait())
    other_normal, other_right = half_system(1 - at.core)
    system_ref[:, :RANK] = own_normal + other_normal
    system_ref[:, RANK:] = own_right + other_right

    loop(1, fib_size, lambda i: tile_copy(i, at.fib).wait_send())
    loop(1, chips, lambda i: chunk_copy(i, at.chip).wait_send())
    loop(1, planes, lambda i: plane_copy(i).wait_send())
    loop(1, chips, lambda i: gather_copy(i, at.chip).wait_send())
    for distance in range(1, WINDOW):
        for copy in shift_copies(distance):
            copy.wait_send()


def normal_system(nodes, interp, table, order, basis, fib_size, pln_size):
    chips = fib_size // 2
    size = PIECES // 2 // chips
    vmem = lambda *shape: pltpu.VMEM(shape, jnp.float32)
    dma = lambda *n: pltpu.SemaphoreType.DMA(n)
    whole = pl.BlockSpec(memory_space=pltpu.VMEM)
    away = pl.BlockSpec(memory_space=pl.ANY)
    return pl.pallas_call(
        functools.partial(step_kernel, fib_size, pln_size),
        out_shape=jax.ShapeDtypeStruct((RANK, 2 * RANK), jnp.float32),
        in_specs=[away, away, pl.BlockSpec(memory_space=pltpu.SMEM), whole, away],
        out_specs=whole,
        scratch_shapes=[
            vmem(*nodes.shape), vmem(*interp.shape), vmem(*basis.shape),
            vmem(WINDOW - 1, CAP, 4 * RANK), vmem(WINDOW, CAP, 4 * RANK), vmem(PIECES, 4, RANK),
            vmem(PIECES, 4, RANK), vmem(PIECES, 4, RANK),
            vmem(size * chips, 4, RANK), vmem(size * chips, 4, RANK), vmem(size * chips, 4, RANK),
            vmem(chips, size, 4, RANK), vmem(size, 4, RANK), vmem(pln_size, size, 4, RANK),
            vmem(size, 4, RANK),
            dma(3), dma(WINDOW - 1, CUTS), dma(WINDOW - 1, CUTS), dma(fib_size), dma(fib_size),
            dma(2), dma(chips), dma(chips), dma(pln_size), dma(pln_size), dma(chips), dma(chips),
            dma(chips), dma(chips),
            pltpu.SemaphoreType.REGULAR((4,)), dma(X_CHIPS), dma(X_CHIPS),
        ],
        compiler_params=pltpu.CompilerParams(collective_id=0, has_side_effects=True),
    )(nodes, interp, table, order, basis)


def per_device(nodal_values, interp_matrix, count_table, slot_order, start_basis):
    system = normal_system(
        nodal_values[0, 0], interp_matrix, jnp.transpose(count_table, (2, 0, 1)), slot_order[0], start_basis,
        lax.axis_size("fib"), lax.axis_size("pln"))
    return eliminate(system)[None, None]


def solution(mesh):
    placed = (P("pln", "fib", None, None), P(), P("pln", None, None), P("pln", "fib", None), P())
    return jax.shard_map(
        per_device,
        mesh=mesh,
        in_specs=placed,
        out_specs=P("pln", "fib", None, None),
        check_vma=False,
    )
```

```python
import functools

import jax
import jax.numpy as jnp
from jax import lax
from jax.experimental import pallas as pl
from jax.experimental.pallas import tpu as pltpu
from jax.sharding import PartitionSpec as P

NX = 768
RANK = 128
WINDOW = 3
CAP = 96
R_ELEM = 192
PIECES = NX // 4
X_CHIPS = 4
CUTS = 4
PIVOTS = 8
HIGHEST = lax.Precision.HIGHEST
MESH_ID = pl.DeviceIdType.MESH


def eliminate_kernel(system_ref, out_ref):
    blocks = RANK // 8
    left = [system_ref[8 * m:8 * m + 8, :RANK] for m in range(blocks)]
    right = [system_ref[8 * m:8 * m + 8, RANK:] for m in range(blocks)]
    rows = lax.broadcasted_iota(jnp.int32, (8, RANK), 0)

    def spread(row):
        return jnp.broadcast_to(row, (8, RANK))

    for k in range(0, RANK, PIVOTS):
        i, r = divmod(k, 8)
        row_left = [spread(left[i][r + a:r + a + 1, :]) for a in range(PIVOTS)]
        row_right = [spread(right[i][r + a:r + a + 1, :]) for a in range(PIVOTS)]
        corner = [[spread(row_left[a][:, k + b:k + b + 1]) if b >= a else None for b in range(PIVOTS)]
                  for a in range(PIVOTS)]
        ratio = [[None] * PIVOTS for _ in range(PIVOTS)]
        inverse = []
        for a in range(PIVOTS):
            inverse.append(1.0 / corner[a][a])
            for b in range(a + 1, PIVOTS):
                ratio[a][b] = corner[a][b] * inverse[a]
                for c in range(b, PIVOTS):
                    corner[b][c] = corner[b][c] - ratio[a][b] * corner[a][c]
                row_left[b] = row_left[b] - ratio[a][b] * row_left[a]
                row_right[b] = row_right[b] - ratio[a][b] * row_right[a]
        for a in range(PIVOTS):
            out_ref[k + a:k + a + 1, :] = (row_right[a] * lax.rsqrt(corner[a][a]))[:1]
        scaled_left = [row_left[a] * inverse[a] for a in range(PIVOTS)]
        scaled_right = [row_right[a] * inverse[a] for a in range(PIVOTS)]
        for m in range(i if r + PIVOTS < 8 else i + 1, blocks):
            factor = []
            for a in range(PIVOTS):
                column = spread(left[m][:, k + a:k + a + 1])
                if m == i:
                    column = jnp.where(rows >= r + PIVOTS, column, 0.0)
                for b in range(a):
                    column = column - ratio[b][a] * factor[b]
                factor.append(column)
            for a in range(PIVOTS):
                left[m] = left[m] - factor[a] * scaled_left[a]
                right[m] = right[m] - factor[a] * scaled_right[a]


def eliminate(system):
    return pl.pallas_call(
        eliminate_kernel,
        out_shape=jax.ShapeDtypeStruct((RANK, system.shape[1] - RANK), jnp.float32),
        in_specs=[pl.BlockSpec(memory_space=pltpu.VMEM)],
        out_specs=pl.BlockSpec(memory_space=pltpu.VMEM),
    )(system)


def remote(src, dst, send_sem, recv_sem, device):
    return pltpu.make_async_remote_copy(
        src_ref=src, dst_ref=dst, send_sem=send_sem, recv_sem=recv_sem,
        device_id=device, device_id_type=MESH_ID,
    )


def loop(low, high, body):
    def step(i, carry):
        body(i)
        return carry
    lax.fori_loop(low, high, step, 0)


class Place:
    def __init__(self, fib_size, pln_size):
        self.fib_size = fib_size
        self.chips = fib_size // 2
        self.depth = self.chips // X_CHIPS
        self.planes = pln_size
        self.fib = lax.axis_index("fib")
        self.pln = lax.axis_index("pln")
        self.core = lax.rem(self.fib, 2)
        self.chip = lax.div(self.fib, 2)
        self.z = lax.div(self.chip, X_CHIPS)
        self.x = lax.rem(self.chip, X_CHIPS)
        self.x_after = [lax.rem(self.x + step, X_CHIPS) for step in range(X_CHIPS)]
        self.x_before = [lax.rem(self.x + X_CHIPS - step, X_CHIPS) for step in range(X_CHIPS)]

    def at_fib(self, fib):
        return {"fib": fib, "pln": self.pln}

    def on_chip(self, chip):
        return self.at_fib(chip * 2 + self.core)

    def other_core(self):
        return self.at_fib(self.chip * 2 + 1 - self.core)

    def along_z(self, step):
        return self.on_chip(lax.rem(self.z + step, self.depth) * X_CHIPS + self.x)

    def along_x(self, step):
        return self.on_chip(self.z * X_CHIPS + self.x_after[step])

    def after(self, distance):
        return lax.rem(self.fib + distance, self.fib_size)

    def in_plane(self, step):
        return {"fib": self.fib, "pln": lax.rem(self.pln + step, self.planes)}

    def over_depth(self, row, far_first):
        if far_first:
            skip = (self.depth // 2 - 2) % (self.depth - 1)
            loop(0, self.depth - 1, lambda n: row(lax.rem(n + skip, self.depth - 1) + 1, True))
            row(0, False)
        else:
            row(0, False)
            loop(1, self.depth, lambda n: row(n, True))

    def row_of_chips(self, body):
        def row(z_step, with_own=True):
            ahead = lax.rem(self.z + z_step, self.depth) * X_CHIPS
            behind = lax.rem(self.z + self.depth - z_step, self.depth) * X_CHIPS
            for x_step in range(0 if with_own else 1, X_CHIPS):
                body(z_step * X_CHIPS + x_step, ahead + self.x_after[x_step], behind + self.x_before[x_step])
        return row

    def each_chip(self, body, far_first=False):
        self.over_depth(self.row_of_chips(body), far_first)

    def each_device(self, body, far_first=False):
        def row(z_step, with_own):
            ahead = lax.rem(self.z + z_step, self.depth) * X_CHIPS
            for x_step in range(X_CHIPS):
                for turn in range(2):
                    if with_own or x_step or turn:
                        core = self.core if turn == 0 else 1 - self.core
                        body((z_step * X_CHIPS + x_step) * 2 + turn, (ahead + self.x_after[x_step]) * 2 + core)
        self.over_depth(row, far_first)


def pair(value):
    high = value.astype(jnp.bfloat16)
    return high, (value - high.astype(jnp.float32)).astype(jnp.bfloat16)


def mult(left, right):
    return jnp.dot(left, right, preferred_element_type=jnp.float32)


def mult3(left, right, contract=1):
    dims = (((contract,), (0,)), ((), ()))
    (left_high, left_low), (right_high, right_low) = pair(left), pair(right)

    def product(a, b):
        return lax.dot_general(a, b, dims, preferred_element_type=jnp.float32)

    return product(left_high, right_high) + (product(left_high, right_low) + product(left_low, right_high))


def gram(left, right):
    return lax.dot_general(left, right, (((0,), (0,)), ((), ())), precision=HIGHEST,
                           preferred_element_type=jnp.float32)


def step_kernel(fib_size, pln_size, nodes_hbm, interp_hbm, table_ref, order_ref, basis_hbm, system_ref,
                nodes_ref, interp_ref, basis_ref, outgoing, incoming, brick, field_ref, image_ref, part, other,
                half, chip_parts, chunk_sum, plane_parts, chunk_done, load_sems, shift_send, shift_recv,
                tile_send, tile_recv, core_sems, chip_send, chip_recv, plane_send, plane_recv, gather_send,
                gather_recv, relay_send, relay_recv, ready, direct_send, direct_recv):
    at = Place(fib_size, pln_size)
    chips, planes = at.chips, at.planes
    size = PIECES // 2 // chips
    split = size * chips
    run = PIECES // fib_size
    barrier = pltpu.get_barrier_semaphore()
    loads = [pltpu.make_async_copy(nodes_hbm, nodes_ref, load_sems.at[0]),
             pltpu.make_async_copy(interp_hbm, interp_ref, load_sems.at[1]),
             pltpu.make_async_copy(basis_hbm, basis_ref, load_sems.at[2])]

    def greet(device):
        pl.semaphore_signal(barrier, inc=1, device_id=device, device_id_type=MESH_ID)

    reach_z, reach_y = at.depth // 4, planes // 4
    near_z = [at.along_z(step) for n in range(reach_z, 0, -1) for step in (n, at.depth - n)]
    near_y = [at.in_plane(step) for n in range(reach_y, 0, -1) for step in (n, planes - n)]
    line_x = [at.along_x(step) for step in range(1, X_CHIPS)]
    window = [at.at_fib(at.after(step)) for step in (1, 2, fib_size - 1, fib_size - 2)]
    first = near_z + near_y + line_x + window + [at.other_core()]
    for device in first:
        greet(device)
    for load in loads:
        load.start()

    starts = [0]
    for distance in range(WINDOW - 1):
        starts.append(starts[-1] + table_ref[distance, 0, at.after(distance)])
    slots = (lax.broadcasted_iota(jnp.int32, (CAP, WINDOW * CAP), 1)
             - lax.broadcasted_iota(jnp.int32, (CAP, WINDOW * CAP), 0))
    for load in loads:
        load.wait()
    interp_high, interp_low = pair(interp_ref[...])
    nodes_high, nodes_low = pair(nodes_ref[...])

    def shift_copies(distance):
        rows = CAP // CUTS
        return [remote(outgoing.at[distance - 1, pl.ds(cut * rows, rows)],
                       incoming.at[distance, pl.ds(cut * rows, rows)],
                       shift_send.at[distance - 1, cut], shift_recv.at[distance - 1, cut],
                       at.at_fib(at.after(distance))) for cut in range(CUTS)]

    for distance in range(WINDOW - 1, -1, -1):
        if distance == 0:
            high, low = nodes_high[:CAP], nodes_low[:CAP]
        else:
            window = jnp.where(slots == starts[distance], 1.0, 0.0).astype(jnp.bfloat16)
            high = mult(window, nodes_high).astype(jnp.bfloat16)
            low = mult(window, nodes_low).astype(jnp.bfloat16)
        values = mult(high, interp_high) + (mult(high, interp_low) + mult(low, interp_high))
        if distance == 0:
            incoming[0] = values
        else:
            outgoing[distance - 1] = values
            if distance == WINDOW - 1:
                pl.semaphore_wait(barrier, len(first))
            for copy in shift_copies(distance):
                copy.start()

    taken_near = table_ref[1, 0, at.fib]
    taken_far = table_ref[2, 0, at.fib]
    ranks = lax.broadcasted_iota(jnp.int32, (1, R_ELEM), 1)
    source = jnp.where(ranks < taken_far, 2 * CAP + ranks,
                       jnp.where(ranks < taken_far + taken_near, CAP + ranks - taken_far,
                                 ranks - taken_far - taken_near))
    places = lax.broadcasted_iota(jnp.int32, (R_ELEM, R_ELEM), 0)
    chosen = jnp.where(order_ref[...] == places, source.astype(jnp.float32), 0.0)
    chosen = jnp.sum(chosen, axis=1, keepdims=True).astype(jnp.int32)
    select = lax.broadcasted_iota(jnp.int32, (R_ELEM, WINDOW * CAP), 1) == chosen
    select = jnp.where(select, 1.0, 0.0).astype(jnp.bfloat16)

    for pairs in (((0, near_z[:2]), (1, near_y[:2])), ((2, line_x),), ((3, [at.other_core()]),)):
        for slot, others in pairs:
            for device in others:
                pl.semaphore_signal(ready.at[slot], inc=1, device_id=device, device_id_type=MESH_ID)
        for slot, others in pairs:
            pl.semaphore_wait(ready.at[slot], len(others))

    for distance in range(WINDOW - 1, 0, -1):
        for copy in shift_copies(distance):
            copy.wait_recv()
    rows = incoming[...].reshape(WINDOW * CAP, 4 * RANK)
    high, low = pair(rows)
    values = mult(select, high) + mult(select, low)
    for l in range(4):
        brick[:, l, :] = values[:, l * RANK:(l + 1) * RANK]

    def own_pieces(fib):
        return pl.ds(fib * run, run)

    def tile_copy(i, peer):
        return remote(brick.at[own_pieces(peer)], field_ref.at[own_pieces(at.fib)], tile_send.at[i],
                      tile_recv.at[i], at.at_fib(peer))

    at.each_device(lambda i, peer: tile_copy(i, peer).start(), far_first=True)
    field_ref[own_pieces(at.fib)] = brick[own_pieces(at.fib)]
    loop(1, fib_size, lambda i: tile_copy(i, at.fib).wait_recv())

    coefficients = mult3(field_ref[...].reshape(NX, RANK), basis_ref[...], 0)

    def partial_image(core):
        rows = field_ref[pl.ds(core * split, split)].reshape(NX // 2, RANK)
        return mult3(rows, coefficients).reshape(split, 4, RANK)

    part[...] = partial_image(1 - at.core)
    swap = remote(part, other, core_sems.at[0], core_sems.at[1], at.other_core())
    swap.start()
    half[...] = partial_image(at.core)
    swap.wait()
    half[...] += other[...]

    def chunk_copy(i, chip):
        return remote(half.at[pl.ds(chip * size, size)], chip_parts.at[i], chip_send.at[i], chip_recv.at[i],
                      at.on_chip(chip))

    at.each_chip(lambda i, chip, back: chunk_copy(i, chip).start(), far_first=True)
    chunk_sum[...] = half[pl.ds(at.chip * size, size)]

    def add_chunk(i):
        chunk_copy(i, at.chip).wait_recv()
        chunk_sum[...] += chip_parts[i]

    loop(1, chips, add_chunk)

    def plane_copy(i):
        return remote(chunk_sum, plane_parts.at[i], plane_send.at[i], plane_recv.at[i], at.in_plane(i))

    loop(1, planes, lambda i: plane_copy(i).start())
    chunk_done[...] = chunk_sum[...]

    def add_plane(i):
        plane_copy(i).wait_recv()
        chunk_done[...] += plane_parts[i]

    loop(1, planes, add_plane)

    def place_of(chip):
        return pl.ds(at.core * split + chip * size, size)

    def gather_copy(i, chip):
        return remote(chunk_done, image_ref.at[place_of(at.chip)], gather_send.at[i], gather_recv.at[i],
                      at.on_chip(chip))

    def relay_copy(i, source, chip):
        return remote(source, image_ref.at[place_of(chip)], relay_send.at[i], relay_recv.at[i], at.other_core())

    far = at.depth // 2

    def direct_copy(i, chip):
        return remote(chunk_done, image_ref.at[place_of(at.chip)], direct_send.at[i], direct_recv.at[i],
                      at.at_fib(chip * 2 + 1 - at.core))

    def send_far(i, chip, back):
        gather_copy(i, chip).start()
        direct_copy(i - far * X_CHIPS, chip).start()

    def other_rows(row):
        loop(far + 1, at.depth, row)
        loop(1, far, row)
        row(0, False)

    at.row_of_chips(send_far)(far)
    other_rows(at.row_of_chips(lambda i, chip, back: gather_copy(i, chip).start()))
    relay_copy(0, chunk_done, at.chip).start()
    image_ref[place_of(at.chip)] = chunk_done[...]

    def pass_on(i, chip, back):
        gather_copy(i, chip).wait_recv()
        relay_copy(i, image_ref.at[place_of(back)], back).start()

    row = at.row_of_chips(pass_on)
    row(0, False)
    loop(1, far, row)
    loop(far + 1, at.depth, row)
    loop(far * X_CHIPS, (far + 1) * X_CHIPS, lambda i: gather_copy(i, at.chip).wait_recv())

    def half_system(core):
        image = image_ref[pl.ds(core * split, split)].reshape(NX // 2, RANK)
        field = field_ref[pl.ds(core * split, split)].reshape(NX // 2, RANK)
        return gram(image, image), mult3(image, field, 0)

    own_normal, own_right = half_system(at.core)
    for low, high in ((0, far * X_CHIPS), ((far + 1) * X_CHIPS, chips)):
        loop(low, high, lambda i: relay_copy(i, chunk_done, at.chip).wait())
    loop(0, X_CHIPS, lambda i: direct_copy(i, at.chip).wait())
    other_normal, other_right = half_system(1 - at.core)
    system_ref[:, :RANK] = own_normal + other_normal
    system_ref[:, RANK:] = own_right + other_right

    loop(1, fib_size, lambda i: tile_copy(i, at.fib).wait_send())
    loop(1, chips, lambda i: chunk_copy(i, at.chip).wait_send())
    loop(1, planes, lambda i: plane_copy(i).wait_send())
    loop(1, chips, lambda i: gather_copy(i, at.chip).wait_send())
    for distance in range(1, WINDOW):
        for copy in shift_copies(distance):
            copy.wait_send()


def normal_system(nodes, interp, table, order, basis, fib_size, pln_size):
    chips = fib_size // 2
    size = PIECES // 2 // chips
    vmem = lambda *shape: pltpu.VMEM(shape, jnp.float32)
    dma = lambda *n: pltpu.SemaphoreType.DMA(n)
    whole = pl.BlockSpec(memory_space=pltpu.VMEM)
    away = pl.BlockSpec(memory_space=pl.ANY)
    return pl.pallas_call(
        functools.partial(step_kernel, fib_size, pln_size),
        out_shape=jax.ShapeDtypeStruct((RANK, 2 * RANK), jnp.float32),
        in_specs=[away, away, pl.BlockSpec(memory_space=pltpu.SMEM), whole, away],
        out_specs=whole,
        scratch_shapes=[
            vmem(*nodes.shape), vmem(*interp.shape), vmem(*basis.shape),
            vmem(WINDOW - 1, CAP, 4 * RANK), vmem(WINDOW, CAP, 4 * RANK), vmem(PIECES, 4, RANK),
            vmem(PIECES, 4, RANK), vmem(PIECES, 4, RANK),
            vmem(size * chips, 4, RANK), vmem(size * chips, 4, RANK), vmem(size * chips, 4, RANK),
            vmem(chips, size, 4, RANK), vmem(size, 4, RANK), vmem(pln_size, size, 4, RANK),
            vmem(size, 4, RANK),
            dma(3), dma(WINDOW - 1, CUTS), dma(WINDOW - 1, CUTS), dma(fib_size), dma(fib_size),
            dma(2), dma(chips), dma(chips), dma(pln_size), dma(pln_size), dma(chips), dma(chips),
            dma(chips), dma(chips),
            pltpu.SemaphoreType.REGULAR((4,)), dma(X_CHIPS), dma(X_CHIPS),
        ],
        compiler_params=pltpu.CompilerParams(collective_id=0, has_side_effects=True),
    )(nodes, interp, table, order, basis)


def per_device(nodal_values, interp_matrix, count_table, slot_order, start_basis):
    system = normal_system(
        nodal_values[0, 0], interp_matrix, jnp.transpose(count_table, (2, 0, 1)), slot_order[0], start_basis,
        lax.axis_size("fib"), lax.axis_size("pln"))
    return eliminate(system)[None, None]


def solution(mesh):
    placed = (P("pln", "fib", None, None), P(), P("pln", None, None), P("pln", "fib", None), P())
    return jax.shard_map(
        per_device,
        mesh=mesh,
        in_specs=placed,
        out_specs=P("pln", "fib", None, None),
        check_vma=False,
    )
```
